32 devices in a mesh: brick: 16 (over z, y, x), seed: 2 (over core).
Axes of the slice: x: 2, y: 2, z: 4, core: 2. Of those that a mesh axis runs over, the one named last changes fastest.
Arguments:
- seed_data: float32 [4, 65536], P(None, ('brick', 'seed')), as said below
- block_slot: int32 [512], replicated, may hold values from 0 to 511, as said below
- candidates: int32 [256, 8], P('brick', 'seed'), may hold values from 0 to 511, as said below
- cand_count: int32 [256], P('brick'), may hold values from 1 to 8
- pixel_mass: float32 [256, 512], P('brick'), may hold values from 0.1 to 1
Outputs:
- seed_stats: float32 [4, 65536], P(None, ('brick', 'seed'))
The draws below stay inside these ranges and needn't reach their ends.
Inputs may be any that keep to these rules, and one draw needn't show every extreme that they name: A permutation of the storage positions. Block g is homed in brick g // 32 and stored on the device of brick index block_slot[g] // 32 and seed index (block_slot[g] // 16) % 2. For each brick and seed index, exactly 16 blocks homed in that brick are stored at that seed index; one device stores at most 1 block homed in any one brick, and some devices reach it. `candidates`: row t holds 8 distinct ids of blocks homed in tile t's brick, between (t // 16) * 32 and that plus 32 - 1. `seed_data`: the seeds of a block lie in the region of its home brick: second coordinate between h * 2 and (h + 1) * 2 for home brick h, first between 0 and 1, third between 0 and 8.
All inputs are finite; a program needn't handle non-finite values.
Results may differ from the reference program's by a relative error of at most 0.0003.
Values sent between devices are 32-bit elements; how exact they have to be, the bound alone decides.
No kernel may reach another device: no remote copies, remote signals or barrier semaphores. Data moves between devices by JAX's collectives and lax.ppermute only.
A program may use at most 64 MiB of HBM per device.

```python
import math
import jax
import jax.numpy as jnp
from jax import lax

TILES_X = 1
TILES_Y = 2
TILES_Z = 8
TILE_PIX = 512
K = 8
BLK_DEV = 16
TILES_DEV = 16
TILES = 256
N_BRICK = 16
N_SEED = 2


def layout_tables(key):
    base = jax.random.fold_in(key, 101)
    home_blocks = BLK_DEV * N_SEED
    total_blocks = home_blocks * N_BRICK
    brick_order = jax.random.permutation(jax.random.fold_in(base, 1), N_BRICK).astype(jnp.int32)
    positions = jnp.arange(total_blocks, dtype=jnp.int32)
    owner_brick = positions // home_blocks
    within = positions % home_blocks
    shard_of = within // BLK_DEV
    lane_of = within % BLK_DEV
    home_brick = brick_order[(owner_brick + shard_of * BLK_DEV + lane_of) % N_BRICK]
    subkeys = jax.random.split(jax.random.fold_in(base, 2), N_BRICK)

    def shuffle_one(subkey):
        return jax.random.permutation(subkey, home_blocks).astype(jnp.int32)
    shuffles = jax.vmap(shuffle_one)(subkeys)
    block_ident = home_brick * home_blocks + shuffles[home_brick, within]
    slot_table = jnp.zeros((total_blocks,), jnp.int32).at[block_ident].set(positions)
    return (home_brick, slot_table)


def draw_block_slot(key, part):
    return layout_tables(key)[1]


def draw_seed_data(key, part):
    home_brick, slot_table = layout_tables(key)
    total_blocks = BLK_DEV * N_SEED * N_BRICK
    uniforms = jax.random.uniform(jax.random.fold_in(key, 5), (4, total_blocks, 128), jnp.float32)
    home_float = home_brick.astype(jnp.float32)[:, None]
    point_x = uniforms[0] * TILES_X
    point_y = (home_float + uniforms[1]) * TILES_Y
    point_z = uniforms[2] * TILES_Z
    offsets = jax.random.uniform(jax.random.fold_in(key, 6), (N_BRICK,), jnp.float32, -55.0, 55.0)
    ramp_key = jax.random.fold_in(key, 8)
    ramp_bits = jax.random.randint(jax.random.fold_in(ramp_key, 1), (N_BRICK,), 0, 2).astype(jnp.int32)
    forced = jax.random.randint(jax.random.fold_in(ramp_key, 2), (), 0, N_BRICK).astype(jnp.int32)
    ramp_on = (ramp_bits == 1) | (jnp.arange(N_BRICK, dtype=jnp.int32) == forced)
    ramp_slope = jnp.where(ramp_on, 12.0, 0.0).astype(jnp.float32)
    if TILES_Z >= TILES_X:
        along = point_z
    else:
        along = point_x
    spread = 0.6 * uniforms[3]
    weights = offsets[home_brick][:, None] + spread + ramp_slope[home_brick][:, None] * along
    stacked = jnp.stack([point_x, point_y, point_z, weights])
    return stacked.reshape(4, total_blocks * 128).astype(jnp.float32)


def draw_candidates(key, part):
    home_blocks = BLK_DEV * N_SEED
    tiles_brick = TILES_X * TILES_Y * TILES_Z
    tiles_all = tiles_brick * N_BRICK
    subkeys = jax.random.split(jax.random.fold_in(key, 7), tiles_all)

    def pick_one(subkey):
        return jax.random.permutation(subkey, home_blocks)[:K].astype(jnp.int32)
    chosen = jax.vmap(pick_one)(subkeys)
    brick_of = (jnp.arange(tiles_all, dtype=jnp.int32) // tiles_brick).astype(jnp.int32)
    return (chosen + brick_of[:, None] * home_blocks).astype(jnp.int32)


def plant(entries, own_key, smallest, largest):
    place = [jax.random.randint(jax.random.fold_in(own_key, axis), (), 0, length) for axis, length in enumerate(entries.shape)]
    widest = entries.shape.index(max(entries.shape))
    neighbour = place[:widest] + [(place[widest] + 1) % entries.shape[widest]] + place[widest + 1:]
    return entries.at[tuple(place)].set(smallest).at[tuple(neighbour)].set(largest)


def block_scale(own_key, extent, shards, smallest, largest):
    factor_of, own = 1.0, jax.random.fold_in(own_key, 6)
    for dim, blocks in shards:
        steps = jnp.exp(jax.random.uniform(jax.random.fold_in(own, dim), (blocks,), jnp.float32, smallest / len(shards), largest / len(shards)))
        factor_of = factor_of * jnp.repeat(steps, extent[dim] // blocks).reshape([-1 if axis == dim else 1 for axis in range(len(extent))])
    return factor_of


def setup_inputs(seed: int = 0) -> dict:
    splits = jax.random.split(jax.random.key(seed), 6)
    seed_data = draw_seed_data(jax.random.fold_in(splits[5], 71), 0)
    block_slot = draw_block_slot(jax.random.fold_in(splits[5], 71), 0)
    candidates = draw_candidates(jax.random.fold_in(splits[5], 71), 0)
    cand_count = plant(jax.random.randint(splits[3], (TILES,), 1, K + 1), jax.random.fold_in(splits[3], 1), 1, K).astype(jnp.int32)
    pixel_mass = jnp.clip(jnp.exp(math.log(1.0) - 2.3025851 * jax.random.uniform(splits[4], (TILES, TILE_PIX), jnp.float32) ** block_scale(splits[4], (TILES, TILE_PIX), ((0, 16),), -0.2, 0.2)), 0.1, 1.0)
    return {"seed_data": seed_data, "block_slot": block_slot, "candidates": candidates, "cand_count": cand_count, "pixel_mass": pixel_mass}


blur_eps = 0.5
far_score = -1.0e30


def pixel_points(brick_ids, tile_ids):
    within = jnp.arange(512, dtype=jnp.int32)
    tile_x = tile_ids // (TILES_Y * TILES_Z)
    tile_y = (tile_ids // TILES_Z) % TILES_Y
    tile_z = tile_ids % TILES_Z
    offset_x = ((within // 64).astype(jnp.float32) + 0.5) / 8.0
    offset_y = (((within // 8) % 8).astype(jnp.float32) + 0.5) / 8.0
    offset_z = ((within % 8).astype(jnp.float32) + 0.5) / 8.0
    point_x = tile_x.astype(jnp.float32)[:, None] + offset_x[None, :]
    point_y = (brick_ids * TILES_Y + tile_y).astype(jnp.float32)[:, None] + offset_y[None, :]
    point_z = tile_z.astype(jnp.float32)[:, None] + offset_z[None, :]
    return jnp.stack([point_x, point_y, point_z])


def tile_scores(points, seed_cols, valid_cols):
    differ = points[0][:, :, None] - seed_cols[0][:, None, :]
    distance = differ * differ
    differ = points[1][:, :, None] - seed_cols[1][:, None, :]
    distance = distance + differ * differ
    differ = points[2][:, :, None] - seed_cols[2][:, None, :]
    distance = distance + differ * differ
    scores = (seed_cols[3][:, None, :] - distance) / blur_eps
    return jnp.where(valid_cols[:, None, :], scores, far_score)


def reference(seed_data, block_slot, candidates, cand_count, pixel_mass):
    total_blocks = block_slot.shape[0]
    stored = seed_data.reshape(4, total_blocks, 128)
    by_ident = stored[:, block_slot, :]
    tile_total = candidates.shape[0]
    group_size = math.gcd(tile_total, 16)
    step_count = tile_total // group_size
    slot_cols = K * 128

    def advance(totals, step_index):
        first_tile = step_index * group_size
        tile_ids = first_tile + jnp.arange(group_size, dtype=jnp.int32)
        points = pixel_points(tile_ids // TILES_DEV, tile_ids % TILES_DEV)
        chosen = lax.dynamic_slice_in_dim(candidates, first_tile, group_size)
        live_count = lax.dynamic_slice_in_dim(cand_count, first_tile, group_size)
        seed_cols = by_ident[:, chosen.reshape(-1), :].reshape(4, group_size, slot_cols)
        valid_slot = jnp.arange(K, dtype=jnp.int32)[None, :] < live_count[:, None]
        valid_cols = jnp.repeat(valid_slot, 128, axis=1)
        scores = tile_scores(points, seed_cols, valid_cols)
        pixel_peak = jnp.max(scores, axis=2)
        raw_share = jnp.where(valid_cols[:, None, :], jnp.exp(scores - pixel_peak[:, :, None]), 0.0)
        pixel_total = jnp.sum(raw_share, axis=2)
        shares = raw_share / pixel_total[:, :, None]
        pixel_weight = lax.dynamic_slice_in_dim(pixel_mass, first_tile, group_size)
        features = jnp.stack([pixel_weight, pixel_weight * points[0], pixel_weight * points[1], pixel_weight * points[2]])
        moments = jnp.einsum("fgi,gic->fgc", features, shares, precision=lax.Precision.HIGHEST)
        totals = totals.at[:, chosen.reshape(-1), :].add(moments.reshape(4, group_size * K, 128))
        return totals, None

    start_totals = jnp.zeros((4, total_blocks, 128), jnp.float32)
    totals, unused = lax.scan(advance, start_totals, jnp.arange(step_count, dtype=jnp.int32))
    mass_row = totals[0]
    moment_rows = totals[1:4] - mass_row[None] * by_ident[0:3]
    stats_by_ident = jnp.concatenate([mass_row[None], moment_rows], axis=0)
    placed = jnp.zeros_like(stats_by_ident).at[:, block_slot, :].set(stats_by_ident)
    return placed.reshape(4, total_blocks * 128)
```

```python
import functools

import jax
import jax.numpy as jnp
from jax import lax
from jax.experimental import pallas as pl
from jax.experimental.pallas import tpu as pltpu
from jax.sharding import PartitionSpec as P

TILES_Y = 2
TILES_Z = 8

LOG2E = 1.4426950408889634
LIFT = 40.0
DEAD = -1e30
CHUNK = 4


def stored_lane(slots, home, lane_count, home_blocks, device_index):
    per_row = 128 // home_blocks
    row = slots[home // per_row : home // per_row + 1, :]
    lanes = lax.broadcasted_iota(jnp.int32, (1, 128), 1)
    shift = lane_count.bit_length() - 1
    first = (home % per_row) * home_blocks
    found = (row >> shift == device_index) & (lanes >= first) & (lanes < first + home_blocks)
    return jnp.max(jnp.where(found, row & (lane_count - 1), -1))


def pack_kernel(sizes, slots_ref, seeds_ref, out_ref):
    brick_size, seed_size, lane_count, home_blocks = sizes
    device_index = lax.axis_index("brick") * seed_size + lax.axis_index("seed")
    slots = slots_ref[...]
    for home in range(brick_size):
        lane = stored_lane(slots, home, lane_count, home_blocks, device_index)
        first = pl.multiple_of(jnp.maximum(lane, 0) * 128, 128)
        block = jnp.where(lane >= 0, seeds_ref[:, pl.ds(first, 128)], 0.0)
        for shard in range(seed_size):
            out_ref[home * seed_size + shard] = block


def place_kernel(sizes, slots_ref, partial_ref, out_ref):
    brick_size, seed_size, lane_count, home_blocks = sizes
    device_index = lax.axis_index("brick") * seed_size + lax.axis_index("seed")
    slots = slots_ref[...]
    for home in range(brick_size):
        lane = stored_lane(slots, home, lane_count, home_blocks, device_index)
        block = partial_ref[home * seed_size]
        for shard in range(1, seed_size):
            block = block + partial_ref[home * seed_size + shard]

        def store(lane=lane, block=block):
            first = pl.multiple_of(jnp.maximum(lane, 0) * 128, 128)
            out_ref[:, pl.ds(first, 128)] = block

        pl.when(lane >= 0)(store)


def split(value):
    high = value.astype(jnp.bfloat16)
    low = (value - high.astype(jnp.float32)).astype(jnp.bfloat16)
    return high, low


def main_kernel(tiles, source_ref, weight_ref, seeds_ref, out_ref, score_ref, za_ref, zs_ref, xy_ref):
    source_count = seeds_ref.shape[0]
    slot_count = source_ref.shape[1]
    chunk_count = source_count // CHUNK
    rows = tiles * 8
    first_tile = lax.axis_index("seed") * tiles
    tile_x = first_tile // (TILES_Y * TILES_Z)
    tile_y = lax.axis_index("brick") * TILES_Y + first_tile // TILES_Z % TILES_Y
    tile_z = first_tile % TILES_Z
    centre_x = tile_x.astype(jnp.float32) + 0.5
    centre_y = tile_y.astype(jnp.float32) + 0.5
    base_z = tile_z.astype(jnp.float32) + 0.5
    centre_z = base_z + lax.broadcasted_iota(jnp.int32, (tiles, 128), 0).astype(jnp.float32)
    step8 = (lax.broadcasted_iota(jnp.int32, (8, 128), 0).astype(jnp.float32) - 3.5) / 8.0

    sources = source_ref[...]
    slot_source = [jnp.broadcast_to(sources[:, k : k + 1], (tiles, 128)) for k in range(slot_count)]

    def near(block):
        off_x = jnp.clip(seeds_ref[block, 0:1, :] - centre_x, -8.0, 8.0)
        off_y = jnp.clip(seeds_ref[block, 1:2, :] - centre_y, -8.0, 8.0)
        return off_x, off_y

    def centre_scores(block, peak):
        off_x, off_y = near(block)
        off_z = seeds_ref[block, 2:3, :] - centre_z
        score = (seeds_ref[block, 3:4, :] - (off_x * off_x + off_y * off_y)) - off_z * off_z
        live = slot_source[0] == block
        for k in range(1, slot_count):
            live = live | (slot_source[k] == block)
        score = jnp.where(live, score, DEAD)
        score_ref[block] = score
        return jnp.maximum(peak, score)

    peak = lax.fori_loop(
        0, source_count, centre_scores, jnp.full((tiles, 128), DEAD, jnp.float32), unroll=8
    )
    peak = jnp.max(peak, axis=1, keepdims=True)

    def factors(chunk, totals):
        for i in range(CHUNK):
            block = chunk * CHUNK + i
            cols = slice(i * 128, (i + 1) * 128)
            off_x, off_y = near(block)
            base = (score_ref[block] - peak) * (2.0 * LOG2E) + LIFT * LOG2E
            slope_z = (seeds_ref[block, 2:3, :] - centre_z) * (4.0 * LOG2E)
            za = jnp.concatenate(
                [jnp.exp2(base[t : t + 1] + step8 * slope_z[t : t + 1]) for t in range(tiles)], axis=0
            )
            za_ref[block] = za
            high, low = split(za)
            zs_ref[chunk, 0:rows, cols] = high
            zs_ref[chunk, rows : 2 * rows, cols] = low
            slope_x = off_x * (4.0 * LOG2E)
            part_y = step8 * (off_y * (4.0 * LOG2E))
            xy = jnp.concatenate(
                [jnp.exp2(slope_x * ((ix - 3.5) / 8.0) + part_y) for ix in range(8)], axis=0
            )
            high, low = split(xy)
            xy_ref[chunk, 0:64, cols] = high
            xy_ref[chunk, 64:128, cols] = low
        return totals + lax.dot_general(
            zs_ref[chunk], xy_ref[chunk], (((1,), (1,)), ((), ())), preferred_element_type=jnp.float32
        )

    totals = lax.fori_loop(0, chunk_count, factors, jnp.zeros((2 * rows, 128), jnp.float32))
    totals = totals[0:rows] + totals[rows : 2 * rows]
    totals = totals + pltpu.roll(totals, 64, 1)
    ratio = weight_ref[...] / totals
    lanes = lax.broadcasted_iota(jnp.int32, (rows, 128), 1)
    step_x = (((lanes >> 3) & 7).astype(jnp.float32) - 3.5) / 8.0
    step_y = ((lanes & 7).astype(jnp.float32) - 3.5) / 8.0
    high, low = split(jnp.concatenate([ratio, ratio * step_x, ratio * step_y], axis=0))
    left = jnp.concatenate([high, low], axis=1)
    pixel_z = jnp.concatenate([step8 + (base_z + t) for t in range(tiles)], axis=0)

    def over_pixels(value):
        value = value.reshape(tiles, 8, 128)
        return jnp.sum(jnp.sum(value, axis=0), axis=0, keepdims=True)

    def moments(chunk, carry):
        right = xy_ref[chunk]
        pulled = jnp.dot(left, jnp.concatenate([right, right], axis=0), preferred_element_type=jnp.float32)
        for i in range(CHUNK):
            block = chunk * CHUNK + i
            cols = slice(i * 128, (i + 1) * 128)
            za = za_ref[block]
            share = za * pulled[0:rows, cols]
            mass = over_pixels(share)
            sum_z = over_pixels(share * pixel_z)
            sum_x = over_pixels(za * pulled[rows : 2 * rows, cols])
            sum_y = over_pixels(za * pulled[2 * rows : 3 * rows, cols])
            off_x, off_y = near(block)
            out_ref[block, 0:1, :] = mass
            out_ref[block, 1:2, :] = sum_x - off_x * mass
            out_ref[block, 2:3, :] = sum_y - off_y * mass
            out_ref[block, 3:4, :] = sum_z - seeds_ref[block, 2:3, :] * mass
        return carry

    lax.fori_loop(0, chunk_count, moments, 0)


def body(seed_data, block_slot, candidates, cand_count, pixel_mass):
    shard_index = lax.axis_index("seed")
    brick_size = lax.axis_size("brick")
    seed_size = lax.axis_size("seed")
    device_count = brick_size * seed_size
    lane_count = seed_data.shape[1] // 128
    home_blocks = lane_count * seed_size
    tile_count = candidates.shape[0]
    tiles = tile_count // seed_size
    assert tiles * seed_size == tile_count and TILES_Z % tiles == 0
    assert 128 % home_blocks == 0 and lane_count & (lane_count - 1) == 0
    assert device_count % CHUNK == 0
    sizes = (brick_size, seed_size, lane_count, home_blocks)
    vmem = pl.BlockSpec(memory_space=pltpu.VMEM)
    panel = jax.ShapeDtypeStruct((device_count, 4, 128), jnp.float32)
    params = pltpu.CompilerParams(vmem_limit_bytes=60 << 20)

    slots = block_slot.reshape(-1, 128)
    outgoing = pl.pallas_call(
        functools.partial(pack_kernel, sizes),
        out_shape=panel,
        in_specs=[vmem, vmem],
        out_specs=vmem,
        name="pack_seeds",
    )(slots, seed_data)
    incoming = lax.all_to_all(outgoing, ("brick", "seed"), split_axis=0, concat_axis=0, tiled=True)

    chosen = lax.all_gather(candidates, "seed", axis=1, tiled=True)
    first_tile = shard_index * tiles
    chosen = lax.dynamic_slice_in_dim(chosen, first_tile, tiles)
    counts = lax.dynamic_slice_in_dim(cand_count, first_tile, tiles)
    slot_ids = jnp.arange(chosen.shape[1], dtype=jnp.int32)
    source = jnp.where(slot_ids[None, :] < counts[:, None], block_slot[chosen] // lane_count, -1)
    weight = lax.dynamic_slice_in_dim(pixel_mass, first_tile, tiles)
    weight = weight.reshape(tiles, 64, 8).transpose(0, 2, 1).reshape(tiles * 8, 64)
    weight = jnp.concatenate([weight, weight], axis=1)

    partial = pl.pallas_call(
        functools.partial(main_kernel, tiles),
        out_shape=panel,
        in_specs=[vmem, vmem, vmem],
        out_specs=vmem,
        scratch_shapes=[
            pltpu.VMEM((device_count, tiles, 128), jnp.float32),
            pltpu.VMEM((device_count, tiles * 8, 128), jnp.float32),
            pltpu.VMEM((device_count // CHUNK, tiles * 16, CHUNK * 128), jnp.bfloat16),
            pltpu.VMEM((device_count // CHUNK, 128, CHUNK * 128), jnp.bfloat16),
        ],
        compiler_params=params,
        name="brick_moments",
    )(source, weight, incoming)
    returned = lax.all_to_all(partial, ("brick", "seed"), split_axis=0, concat_axis=0, tiled=True)
    return pl.pallas_call(
        functools.partial(place_kernel, sizes),
        out_shape=jax.ShapeDtypeStruct(seed_data.shape, jnp.float32),
        in_specs=[vmem, vmem],
        out_specs=vmem,
        name="place_stats",
    )(slots, returned)


def solution(mesh):
    placed = (P(None, ("brick", "seed")), P(), P("brick", "seed"), P("brick"), P("brick", None))
    return jax.shard_map(
        body, mesh=mesh, in_specs=placed, out_specs=P(None, ("brick", "seed")), check_vma=False
    )
```

```python
import functools

import jax
import jax.numpy as jnp
from jax import lax
from jax.experimental import pallas as pl
from jax.experimental.pallas import tpu as pltpu
from jax.sharding import PartitionSpec as P

TILES_Y = 2
TILES_Z = 8

LOG2E = 1.4426950408889634
LIFT = 40.0
DEAD = -1e30
CHUNK = 4


def stored_lane(slots, home, lane_count, home_blocks, device_index):
    per_row = 128 // home_blocks
    row = slots[home // per_row : home // per_row + 1, :]
    lanes = lax.broadcasted_iota(jnp.int32, (1, 128), 1)
    shift = lane_count.bit_length() - 1
    first = (home % per_row) * home_blocks
    found = (row >> shift == device_index) & (lanes >= first) & (lanes < first + home_blocks)
    return jnp.max(jnp.where(found, row & (lane_count - 1), -1))


def pack_kernel(sizes, slots_ref, seeds_ref, out_ref):
    brick_size, seed_size, lane_count, home_blocks = sizes
    device_index = lax.axis_index("brick") * seed_size + lax.axis_index("seed")
    slots = slots_ref[...]
    for home in range(brick_size):
        lane = stored_lane(slots, home, lane_count, home_blocks, device_index)
        first = pl.multiple_of(jnp.maximum(lane, 0) * 128, 128)
        block = jnp.where(lane >= 0, seeds_ref[:, pl.ds(first, 128)], 0.0)
        for shard in range(seed_size):
            out_ref[home * seed_size + shard] = block


def place_kernel(sizes, slots_ref, partial_ref, out_ref):
    brick_size, seed_size, lane_count, home_blocks = sizes
    device_index = lax.axis_index("brick") * seed_size + lax.axis_index("seed")
    slots = slots_ref[...]
    rows = lax.broadcasted_iota(jnp.int32, slots.shape, 0)
    lanes = lax.broadcasted_iota(jnp.int32, slots.shape, 1)
    home = (rows * 128 + lanes) >> (home_blocks.bit_length() - 1)
    homes = [
        jnp.max(jnp.where(slots == device_index * lane_count + lane, home, 0)) for lane in range(lane_count)
    ]
    for lane in range(lane_count):
        block = partial_ref[homes[lane] * seed_size]
        for shard in range(1, seed_size):
            block = block + partial_ref[homes[lane] * seed_size + shard]
        out_ref[:, lane * 128 : (lane + 1) * 128] = block


def split(value):
    high = value.astype(jnp.bfloat16)
    low = (value - high.astype(jnp.float32)).astype(jnp.bfloat16)
    return high, low


def main_kernel(tiles, source_ref, weight_ref, seeds_ref, out_ref, score_ref, za_ref, zs_ref, xy_ref):
    source_count = seeds_ref.shape[0]
    slot_count = source_ref.shape[1]
    chunk_count = source_count // CHUNK
    rows = tiles * 8
    first_tile = lax.axis_index("seed") * tiles
    tile_x = first_tile // (TILES_Y * TILES_Z)
    tile_y = lax.axis_index("brick") * TILES_Y + first_tile // TILES_Z % TILES_Y
    tile_z = first_tile % TILES_Z
    centre_x = tile_x.astype(jnp.float32) + 0.5
    centre_y = tile_y.astype(jnp.float32) + 0.5
    base_z = tile_z.astype(jnp.float32) + 0.5
    centre_z = base_z + lax.broadcasted_iota(jnp.int32, (tiles, 128), 0).astype(jnp.float32)
    step8 = (lax.broadcasted_iota(jnp.int32, (8, 128), 0).astype(jnp.float32) - 3.5) / 8.0

    sources = source_ref[...]
    slot_source = [jnp.broadcast_to(sources[:, k : k + 1], (tiles, 128)) for k in range(slot_count)]

    def near(block):
        off_x = jnp.clip(seeds_ref[block, 0:1, :] - centre_x, -8.0, 8.0)
        off_y = jnp.clip(seeds_ref[block, 1:2, :] - centre_y, -8.0, 8.0)
        return off_x, off_y

    def centre_scores(block, peak):
        off_x, off_y = near(block)
        off_z = seeds_ref[block, 2:3, :] - centre_z
        score = (seeds_ref[block, 3:4, :] - (off_x * off_x + off_y * off_y)) - off_z * off_z
        live = slot_source[0] == block
        for k in range(1, slot_count):
            live = live | (slot_source[k] == block)
        score = jnp.where(live, score, DEAD)
        score_ref[block] = score
        return jnp.maximum(peak, score)

    peak = lax.fori_loop(
        0, source_count, centre_scores, jnp.full((tiles, 128), DEAD, jnp.float32), unroll=8
    )
    peak = jnp.max(peak, axis=1, keepdims=True)

    def factors(chunk, totals):
        for i in range(CHUNK):
            block = chunk * CHUNK + i
            cols = slice(i * 128, (i + 1) * 128)
            off_x, off_y = near(block)
            base = (score_ref[block] - peak) * (2.0 * LOG2E) + LIFT * LOG2E
            slope_z = (seeds_ref[block, 2:3, :] - centre_z) * (4.0 * LOG2E)
            za = jnp.concatenate(
                [jnp.exp2(base[t : t + 1] + step8 * slope_z[t : t + 1]) for t in range(tiles)], axis=0
            )
            za_ref[block] = za
            high, low = split(za)
            zs_ref[chunk, 0:rows, cols] = high
            zs_ref[chunk, rows : 2 * rows, cols] = low
            slope_x = off_x * (4.0 * LOG2E)
            part_y = step8 * (off_y * (4.0 * LOG2E))
            xy = jnp.concatenate(
                [jnp.exp2(slope_x * ((ix - 3.5) / 8.0) + part_y) for ix in range(8)], axis=0
            )
            high, low = split(xy)
            xy_ref[chunk, 0:64, cols] = high
            xy_ref[chunk, 64:128, cols] = low
        return totals + lax.dot_general(
            zs_ref[chunk], xy_ref[chunk], (((1,), (1,)), ((), ())), preferred_element_type=jnp.float32
        )

    totals = lax.fori_loop(0, chunk_count, factors, jnp.zeros((2 * rows, 128), jnp.float32))
    totals = totals[0:rows] + totals[rows : 2 * rows]
    totals = totals + pltpu.roll(totals, 64, 1)
    ratio = weight_ref[...] / totals
    lanes = lax.broadcasted_iota(jnp.int32, (rows, 128), 1)
    step_x = (((lanes >> 3) & 7).astype(jnp.float32) - 3.5) / 8.0
    step_y = ((lanes & 7).astype(jnp.float32) - 3.5) / 8.0
    high, low = split(jnp.concatenate([ratio, ratio * step_x, ratio * step_y], axis=0))
    left = jnp.concatenate([high, low], axis=1)
    pixel_z = jnp.concatenate([step8 + (base_z + t) for t in range(tiles)], axis=0)

    def over_pixels(value):
        value = value.reshape(tiles, 8, 128)
        return jnp.sum(jnp.sum(value, axis=0), axis=0, keepdims=True)

    def moments(chunk, carry):
        right = xy_ref[chunk]
        pulled = jnp.dot(left, jnp.concatenate([right, right], axis=0), preferred_element_type=jnp.float32)
        for i in range(CHUNK):
            block = chunk * CHUNK + i
            cols = slice(i * 128, (i + 1) * 128)
            za = za_ref[block]
            share = za * pulled[0:rows, cols]
            mass = over_pixels(share)
            sum_z = over_pixels(share * pixel_z)
            sum_x = over_pixels(za * pulled[rows : 2 * rows, cols])
            sum_y = over_pixels(za * pulled[2 * rows : 3 * rows, cols])
            off_x, off_y = near(block)
            out_ref[block, 0:1, :] = mass
            out_ref[block, 1:2, :] = sum_x - off_x * mass
            out_ref[block, 2:3, :] = sum_y - off_y * mass
            out_ref[block, 3:4, :] = sum_z - seeds_ref[block, 2:3, :] * mass
        return carry

    lax.fori_loop(0, chunk_count, moments, 0)


def body(seed_data, block_slot, candidates, cand_count, pixel_mass):
    shard_index = lax.axis_index("seed")
    brick_size = lax.axis_size("brick")
    seed_size = lax.axis_size("seed")
    device_count = brick_size * seed_size
    lane_count = seed_data.shape[1] // 128
    home_blocks = lane_count * seed_size
    tile_count = candidates.shape[0]
    tiles = tile_count // seed_size
    assert tiles * seed_size == tile_count and TILES_Z % tiles == 0
    assert 128 % home_blocks == 0 and lane_count & (lane_count - 1) == 0
    assert device_count % CHUNK == 0
    sizes = (brick_size, seed_size, lane_count, home_blocks)
    vmem = pl.BlockSpec(memory_space=pltpu.VMEM)
    panel = pltpu.VMEM((device_count, 4, 128), jnp.float32)
    near = functools.partial(pltpu.with_memory_space_constraint, memory_space=pltpu.VMEM)
    params = pltpu.CompilerParams(vmem_limit_bytes=60 << 20)

    slots = block_slot.reshape(-1, 128)
    outgoing = pl.pallas_call(
        functools.partial(pack_kernel, sizes),
        out_shape=panel,
        in_specs=[vmem, vmem],
        out_specs=vmem,
        name="pack_seeds",
    )(slots, seed_data)
    incoming = lax.all_to_all(outgoing, ("brick", "seed"), split_axis=0, concat_axis=0, tiled=True)

    chosen = lax.all_gather(candidates, "seed", axis=1, tiled=True)
    first_tile = shard_index * tiles
    chosen = lax.dynamic_slice_in_dim(chosen, first_tile, tiles)
    counts = lax.dynamic_slice_in_dim(cand_count, first_tile, tiles)
    slot_ids = jnp.arange(chosen.shape[1], dtype=jnp.int32)
    source = jnp.where(slot_ids[None, :] < counts[:, None], block_slot[chosen] // lane_count, -1)
    weight = lax.dynamic_slice_in_dim(pixel_mass, first_tile, tiles)
    weight = weight.reshape(tiles, 64, 8).transpose(0, 2, 1).reshape(tiles * 8, 64)
    weight = jnp.concatenate([weight, weight], axis=1)

    partial = pl.pallas_call(
        functools.partial(main_kernel, tiles),
        out_shape=panel,
        in_specs=[vmem, vmem, vmem],
        out_specs=vmem,
        scratch_shapes=[
            pltpu.VMEM((device_count, tiles, 128), jnp.float32),
            pltpu.VMEM((device_count, tiles * 8, 128), jnp.float32),
            pltpu.VMEM((device_count // CHUNK, tiles * 16, CHUNK * 128), jnp.bfloat16),
            pltpu.VMEM((device_count // CHUNK, 128, CHUNK * 128), jnp.bfloat16),
        ],
        compiler_params=params,
        name="brick_moments",
    )(near(source), near(weight), near(incoming))
    returned = lax.all_to_all(partial, ("brick", "seed"), split_axis=0, concat_axis=0, tiled=True)
    return pl.pallas_call(
        functools.partial(place_kernel, sizes),
        out_shape=jax.ShapeDtypeStruct(seed_data.shape, jnp.float32),
        in_specs=[vmem, vmem],
        out_specs=vmem,
        name="place_stats",
    )(slots, near(returned))


def solution(mesh):
    placed = (P(None, ("brick", "seed")), P(), P("brick", "seed"), P("brick"), P("brick", None))
    return jax.shard_map(
        body, mesh=mesh, in_specs=placed, out_specs=P(None, ("brick", "seed")), check_vma=False
    )
```

```python
import functools

import jax
import jax.numpy as jnp
from jax import lax
from jax.experimental import pallas as pl
from jax.experimental.pallas import tpu as pltpu
from jax.sharding import PartitionSpec as P

TILES_Y = 2
TILES_Z = 8

LOG2E = 1.4426950408889634
LIFT = 40.0
DEAD = -1e30
CHUNK = 4


def stored_lane(slots, home, lane_count, home_blocks, device_index):
    per_row = 128 // home_blocks
    row = slots[home // per_row : home // per_row + 1, :]
    lanes = lax.broadcasted_iota(jnp.int32, (1, 128), 1)
    shift = lane_count.bit_length() - 1
    first = (home % per_row) * home_blocks
    found = (row >> shift == device_index) & (lanes >= first) & (lanes < first + home_blocks)
    return jnp.max(jnp.where(found, row & (lane_count - 1), -1))


def pack_kernel(sizes, slots_ref, seeds_ref, out_ref):
    brick_size, seed_size, lane_count, home_blocks = sizes
    device_index = lax.axis_index("brick") * seed_size + lax.axis_index("seed")
    slots = slots_ref[...]
    for home in range(brick_size):
        lane = stored_lane(slots, home, lane_count, home_blocks, device_index)
        first = pl.multiple_of(jnp.maximum(lane, 0) * 128, 128)
        block = jnp.where(lane >= 0, seeds_ref[:, pl.ds(first, 128)], 0.0)
        for shard in range(seed_size):
            out_ref[home * seed_size + shard] = block


def prepare_kernel(sizes, tiles, slots_ref, counts_ref, *refs):
    brick_size, seed_size, lane_count, home_blocks = sizes
    panels, (source_ref, homes_ref) = refs[:seed_size], refs[seed_size:]
    brick_index = lax.axis_index("brick")
    shard_index = lax.axis_index("seed")
    shift = lane_count.bit_length() - 1
    slot_count, tile_count = panels[0].shape

    row = brick_index // (128 // home_blocks)
    lanes = lax.broadcasted_iota(jnp.int32, (1, 128), 1)
    ident = jnp.broadcast_to(row * 128 + lanes, (tiles, 128))
    holder = jnp.broadcast_to(slots_ref[pl.ds(row, 1), :] >> shift, (tiles, 128))
    mine = shard_index * tiles + lax.broadcasted_iota(jnp.int32, (tiles, tile_count), 0)
    mine = mine == lax.broadcasted_iota(jnp.int32, (tiles, tile_count), 1)
    counts = counts_ref[...]
    for turn in range(seed_size):
        shard = lax.rem(shard_index + turn, seed_size)
        for k in range(slot_count):
            chosen = jnp.where(shard * slot_count + k < counts, panels[turn][k : k + 1, :], -1)
            chosen = jnp.where(mine, jnp.broadcast_to(chosen, (tiles, tile_count)), -1)
            chosen = jnp.max(chosen, axis=1, keepdims=True)
            source = jnp.max(jnp.where(ident == chosen, holder, -1), axis=1, keepdims=True)
            source_ref[turn * slot_count + k] = jnp.broadcast_to(source, (tiles, 128))

    slots = slots_ref[...]
    rows = lax.broadcasted_iota(jnp.int32, slots.shape, 0)
    lanes = lax.broadcasted_iota(jnp.int32, slots.shape, 1)
    home = (rows * 128 + lanes) >> (home_blocks.bit_length() - 1)
    first = (brick_index * seed_size + shard_index) * lane_count
    for lane in range(lane_count):
        homes_ref[lane] = jnp.max(jnp.where(slots == first + lane, home, 0))


def place_kernel(seed_size, homes_ref, partial_ref, out_ref):
    for lane in range(out_ref.shape[1] // 128):
        first = homes_ref[lane] * seed_size
        block = partial_ref[first]
        for shard in range(1, seed_size):
            block = block + partial_ref[first + shard]
        out_ref[:, lane * 128 : (lane + 1) * 128] = block


def split(value):
    high = value.astype(jnp.bfloat16)
    low = (value - high.astype(jnp.float32)).astype(jnp.bfloat16)
    return high, low


def main_kernel(tiles, source_ref, weight_ref, seeds_ref, out_ref, score_ref, za_ref, zs_ref, xy_ref):
    source_count = seeds_ref.shape[0]
    slot_count = source_ref.shape[0]
    chunk_count = source_count // CHUNK
    rows = tiles * 8
    first_tile = lax.axis_index("seed") * tiles
    tile_x = first_tile // (TILES_Y * TILES_Z)
    tile_y = lax.axis_index("brick") * TILES_Y + first_tile // TILES_Z % TILES_Y
    tile_z = first_tile % TILES_Z
    centre_x = tile_x.astype(jnp.float32) + 0.5
    centre_y = tile_y.astype(jnp.float32) + 0.5
    base_z = tile_z.astype(jnp.float32) + 0.5
    centre_z = base_z + lax.broadcasted_iota(jnp.int32, (tiles, 128), 0).astype(jnp.float32)
    step8 = (lax.broadcasted_iota(jnp.int32, (8, 128), 0).astype(jnp.float32) - 3.5) / 8.0

    slot_source = [source_ref[k] for k in range(slot_count)]

    def near(block):
        off_x = jnp.clip(seeds_ref[block, 0:1, :] - centre_x, -8.0, 8.0)
        off_y = jnp.clip(seeds_ref[block, 1:2, :] - centre_y, -8.0, 8.0)
        return off_x, off_y

    def centre_scores(block, peak):
        off_x, off_y = near(block)
        off_z = seeds_ref[block, 2:3, :] - centre_z
        score = (seeds_ref[block, 3:4, :] - (off_x * off_x + off_y * off_y)) - off_z * off_z
        live = slot_source[0] == block
        for k in range(1, slot_count):
            live = live | (slot_source[k] == block)
        score = jnp.where(live, score, DEAD)
        score_ref[block] = score
        return jnp.maximum(peak, score)

    peak = lax.fori_loop(
        0, source_count, centre_scores, jnp.full((tiles, 128), DEAD, jnp.float32), unroll=8
    )
    peak = jnp.max(peak, axis=1, keepdims=True)

    def factors(chunk, totals):
        for i in range(CHUNK):
            block = chunk * CHUNK + i
            cols = slice(i * 128, (i + 1) * 128)
            off_x, off_y = near(block)
            base = (score_ref[block] - peak) * (2.0 * LOG2E) + LIFT * LOG2E
            slope_z = (seeds_ref[block, 2:3, :] - centre_z) * (4.0 * LOG2E)
            za = jnp.concatenate(
                [jnp.exp2(base[t : t + 1] + step8 * slope_z[t : t + 1]) for t in range(tiles)], axis=0
            )
            za_ref[block] = za
            high, low = split(za)
            zs_ref[chunk, 0:rows, cols] = high
            zs_ref[chunk, rows : 2 * rows, cols] = low
            slope_x = off_x * (4.0 * LOG2E)
            part_y = step8 * (off_y * (4.0 * LOG2E))
            xy = jnp.concatenate(
                [jnp.exp2(slope_x * ((ix - 3.5) / 8.0) + part_y) for ix in range(8)], axis=0
            )
            high, low = split(xy)
            xy_ref[chunk, 0:64, cols] = high
            xy_ref[chunk, 64:128, cols] = low
        return totals + lax.dot_general(
            zs_ref[chunk], xy_ref[chunk], (((1,), (1,)), ((), ())), preferred_element_type=jnp.float32
        )

    totals = lax.fori_loop(0, chunk_count, factors, jnp.zeros((2 * rows, 128), jnp.float32))
    totals = totals[0:rows] + totals[rows : 2 * rows]
    totals = totals + pltpu.roll(totals, 64, 1)
    weight = weight_ref[...]
    ratio = jnp.concatenate([weight, weight], axis=1) / totals
    lanes = lax.broadcasted_iota(jnp.int32, (rows, 128), 1)
    step_x = (((lanes >> 3) & 7).astype(jnp.float32) - 3.5) / 8.0
    step_y = ((lanes & 7).astype(jnp.float32) - 3.5) / 8.0
    high, low = split(jnp.concatenate([ratio, ratio * step_x, ratio * step_y], axis=0))
    left = jnp.concatenate([high, low], axis=1)
    pixel_z = jnp.concatenate([step8 + (base_z + t) for t in range(tiles)], axis=0)

    def over_pixels(value):
        value = value.reshape(tiles, 8, 128)
        return jnp.sum(jnp.sum(value, axis=0), axis=0, keepdims=True)

    def moments(chunk, carry):
        right = xy_ref[chunk]
        pulled = jnp.dot(left, jnp.concatenate([right, right], axis=0), preferred_element_type=jnp.float32)
        for i in range(CHUNK):
            block = chunk * CHUNK + i
            cols = slice(i * 128, (i + 1) * 128)
            za = za_ref[block]
            share = za * pulled[0:rows, cols]
            mass = over_pixels(share)
            sum_z = over_pixels(share * pixel_z)
            sum_x = over_pixels(za * pulled[rows : 2 * rows, cols])
            sum_y = over_pixels(za * pulled[2 * rows : 3 * rows, cols])
            off_x, off_y = near(block)
            out_ref[block, 0:1, :] = mass
            out_ref[block, 1:2, :] = sum_x - off_x * mass
            out_ref[block, 2:3, :] = sum_y - off_y * mass
            out_ref[block, 3:4, :] = sum_z - seeds_ref[block, 2:3, :] * mass
        return carry

    lax.fori_loop(0, chunk_count, moments, 0)


def body(seed_data, block_slot, candidates, cand_count, pixel_mass):
    shard_index = lax.axis_index("seed")
    brick_size = lax.axis_size("brick")
    seed_size = lax.axis_size("seed")
    device_count = brick_size * seed_size
    lane_count = seed_data.shape[1] // 128
    home_blocks = lane_count * seed_size
    tile_count = candidates.shape[0]
    tiles = tile_count // seed_size
    assert tiles * seed_size == tile_count and TILES_Z % tiles == 0
    assert 128 % home_blocks == 0 and lane_count & (lane_count - 1) == 0
    assert device_count % CHUNK == 0
    sizes = (brick_size, seed_size, lane_count, home_blocks)
    vmem = pl.BlockSpec(memory_space=pltpu.VMEM)
    smem = pl.BlockSpec(memory_space=pltpu.SMEM)
    panel = pltpu.VMEM((device_count, 4, 128), jnp.float32)
    near = functools.partial(pltpu.with_memory_space_constraint, memory_space=pltpu.VMEM)
    params = pltpu.CompilerParams(vmem_limit_bytes=60 << 20)

    slots = block_slot.reshape(-1, 128)
    outgoing = pl.pallas_call(
        functools.partial(pack_kernel, sizes),
        out_shape=panel,
        in_specs=[vmem, vmem],
        out_specs=vmem,
        name="pack_seeds",
    )(slots, seed_data)
    incoming = lax.all_to_all(outgoing, ("brick", "seed"), split_axis=0, concat_axis=0, tiled=True)

    own = candidates.T
    panels = [own]
    for turn in range(1, seed_size):
        pairs = [(shard, (shard - turn) % seed_size) for shard in range(seed_size)]
        panels.append(lax.ppermute(own, "seed", pairs))
    slot_total = own.shape[0] * seed_size
    source, homes = pl.pallas_call(
        functools.partial(prepare_kernel, sizes, tiles),
        out_shape=(pltpu.VMEM((slot_total, tiles, 128), jnp.int32), pltpu.SMEM((lane_count,), jnp.int32)),
        in_specs=[vmem] * (2 + seed_size),
        out_specs=(vmem, smem),
        name="prepare",
    )(near(slots), near(cand_count.reshape(1, -1)), *[near(part) for part in panels])
    weight = lax.dynamic_slice_in_dim(pixel_mass, shard_index * tiles, tiles)
    weight = weight.reshape(tiles, 64, 8).transpose(0, 2, 1).reshape(tiles * 8, 64)

    partial = pl.pallas_call(
        functools.partial(main_kernel, tiles),
        out_shape=panel,
        in_specs=[vmem, vmem, vmem],
        out_specs=vmem,
        scratch_shapes=[
            pltpu.VMEM((device_count, tiles, 128), jnp.float32),
            pltpu.VMEM((device_count, tiles * 8, 128), jnp.float32),
            pltpu.VMEM((device_count // CHUNK, tiles * 16, CHUNK * 128), jnp.bfloat16),
            pltpu.VMEM((device_count // CHUNK, 128, CHUNK * 128), jnp.bfloat16),
        ],
        compiler_params=params,
        name="brick_moments",
    )(near(source), near(weight), near(incoming))
    returned = lax.all_to_all(partial, ("brick", "seed"), split_axis=0, concat_axis=0, tiled=True)
    return pl.pallas_call(
        functools.partial(place_kernel, seed_size),
        out_shape=jax.ShapeDtypeStruct(seed_data.shape, jnp.float32),
        in_specs=[smem, vmem],
        out_specs=vmem,
        name="place_stats",
    )(homes, near(returned))


def solution(mesh):
    placed = (P(None, ("brick", "seed")), P(), P("brick", "seed"), P("brick"), P("brick", None))
    return jax.shard_map(
        body, mesh=mesh, in_specs=placed, out_specs=P(None, ("brick", "seed")), check_vma=False
    )
```

```python
import functools

import jax
import jax.numpy as jnp
from jax import lax
from jax.experimental import pallas as pl
from jax.experimental.pallas import tpu as pltpu
from jax.sharding import PartitionSpec as P

TILES_Y = 2
TILES_Z = 8

LOG2E = 1.4426950408889634
LIFT = 40.0
DEAD = -1e30
CHUNK = 4


def stored_lane(slots, home, lane_count, home_blocks, device_index):
    per_row = 128 // home_blocks
    row = slots[home // per_row : home // per_row + 1, :]
    lanes = lax.broadcasted_iota(jnp.int32, (1, 128), 1)
    shift = lane_count.bit_length() - 1
    first = (home % per_row) * home_blocks
    found = (row >> shift == device_index) & (lanes >= first) & (lanes < first + home_blocks)
    return jnp.max(jnp.where(found, row & (lane_count - 1), -1))


def pack_kernel(sizes, slots_ref, seeds_ref, out_ref):
    brick_size, seed_size, lane_count, home_blocks = sizes
    device_index = lax.axis_index("brick") * seed_size + lax.axis_index("seed")
    slots = slots_ref[...]
    for home in range(brick_size):
        lane = stored_lane(slots, home, lane_count, home_blocks, device_index)
        first = pl.multiple_of(jnp.maximum(lane, 0) * 128, 128)
        block = jnp.where(lane >= 0, seeds_ref[:, pl.ds(first, 128)], 0.0)
        for shard in range(seed_size):
            out_ref[home * seed_size + shard] = block


def prepare_kernel(sizes, tiles, slots_ref, counts_ref, *refs):
    brick_size, seed_size, lane_count, home_blocks = sizes
    panels, (source_ref, homes_ref) = refs[:seed_size], refs[seed_size:]
    brick_index = lax.axis_index("brick")
    shard_index = lax.axis_index("seed")
    shift = lane_count.bit_length() - 1
    slot_count, tile_count = panels[0].shape

    row = brick_index // (128 // home_blocks)
    lanes = lax.broadcasted_iota(jnp.int32, (1, 128), 1)
    ident = jnp.broadcast_to(row * 128 + lanes, (tiles, 128))
    holder = jnp.broadcast_to(slots_ref[pl.ds(row, 1), :] >> shift, (tiles, 128))
    mine = shard_index * tiles + lax.broadcasted_iota(jnp.int32, (tiles, tile_count), 0)
    mine = mine == lax.broadcasted_iota(jnp.int32, (tiles, tile_count), 1)
    counts = counts_ref[...]
    for turn in range(seed_size):
        shard = lax.rem(shard_index + turn, seed_size)
        for k in range(slot_count):
            chosen = jnp.where(shard * slot_count + k < counts, panels[turn][k : k + 1, :], -1)
            chosen = jnp.where(mine, jnp.broadcast_to(chosen, (tiles, tile_count)), -1)
            chosen = jnp.max(chosen, axis=1, keepdims=True)
            source = jnp.max(jnp.where(ident == chosen, holder, -1), axis=1, keepdims=True)
            source_ref[turn * slot_count + k] = jnp.broadcast_to(source, (tiles, 128))

    slots = slots_ref[...]
    rows = lax.broadcasted_iota(jnp.int32, slots.shape, 0)
    lanes = lax.broadcasted_iota(jnp.int32, slots.shape, 1)
    home = (rows * 128 + lanes) >> (home_blocks.bit_length() - 1)
    first = (brick_index * seed_size + shard_index) * lane_count
    for lane in range(lane_count):
        homes_ref[lane] = jnp.max(jnp.where(slots == first + lane, home, 0))


def place_kernel(seed_size, homes_ref, partial_ref, out_ref):
    for lane in range(out_ref.shape[1] // 128):
        first = homes_ref[lane] * seed_size
        block = partial_ref[first]
        for shard in range(1, seed_size):
            block = block + partial_ref[first + shard]
        out_ref[:, lane * 128 : (lane + 1) * 128] = block


def split(value):
    high = value.astype(jnp.bfloat16)
    low = (value - high.astype(jnp.float32)).astype(jnp.bfloat16)
    return high, low


def main_kernel(tiles, source_ref, weight_ref, seeds_ref, out_ref, score_ref, za_ref, zs_ref, xy_ref):
    source_count = seeds_ref.shape[0]
    slot_count = source_ref.shape[0]
    chunk_count = source_count // CHUNK
    rows = tiles * 8
    first_tile = lax.axis_index("seed") * tiles
    tile_x = first_tile // (TILES_Y * TILES_Z)
    tile_y = lax.axis_index("brick") * TILES_Y + first_tile // TILES_Z % TILES_Y
    tile_z = first_tile % TILES_Z
    centre_x = tile_x.astype(jnp.float32) + 0.5
    centre_y = tile_y.astype(jnp.float32) + 0.5
    base_z = tile_z.astype(jnp.float32) + 0.5
    centre_z = base_z + lax.broadcasted_iota(jnp.int32, (tiles, 128), 0).astype(jnp.float32)
    step8 = (lax.broadcasted_iota(jnp.int32, (8, 128), 0).astype(jnp.float32) - 3.5) / 8.0

    slot_source = [source_ref[k] for k in range(slot_count)]

    def near(block):
        off_x = jnp.clip(seeds_ref[block, 0:1, :] - centre_x, -8.0, 8.0)
        off_y = jnp.clip(seeds_ref[block, 1:2, :] - centre_y, -8.0, 8.0)
        return off_x, off_y

    def centre_scores(block, peak):
        off_x, off_y = near(block)
        off_z = seeds_ref[block, 2:3, :] - centre_z
        score = (seeds_ref[block, 3:4, :] - (off_x * off_x + off_y * off_y)) - off_z * off_z
        live = slot_source[0] == block
        for k in range(1, slot_count):
            live = live | (slot_source[k] == block)
        score = jnp.where(live, score, DEAD)
        score_ref[block] = score
        return jnp.maximum(peak, score)

    peak = lax.fori_loop(
        0, source_count, centre_scores, jnp.full((tiles, 128), DEAD, jnp.float32), unroll=8
    )
    peak = jnp.max(peak, axis=1, keepdims=True)

    def factors(chunk, totals):
        for i in range(CHUNK):
            block = chunk * CHUNK + i
            cols = slice(i * 128, (i + 1) * 128)
            off_x, off_y = near(block)
            base = (score_ref[block] - peak) * (2.0 * LOG2E) + LIFT * LOG2E
            slope_z = (seeds_ref[block, 2:3, :] - centre_z) * (4.0 * LOG2E)
            za = jnp.concatenate(
                [jnp.exp2(base[t : t + 1] + step8 * slope_z[t : t + 1]) for t in range(tiles)], axis=0
            )
            za_ref[block] = za
            high, low = split(za)
            zs_ref[chunk, 0:rows, cols] = high
            zs_ref[chunk, rows : 2 * rows, cols] = low
            slope_x = off_x * (4.0 * LOG2E)
            part_y = step8 * (off_y * (4.0 * LOG2E))
            xy = jnp.concatenate(
                [jnp.exp2(slope_x * ((ix - 3.5) / 8.0) + part_y) for ix in range(8)], axis=0
            )
            high, low = split(xy)
            xy_ref[chunk, 0:64, cols] = high
            xy_ref[chunk, 64:128, cols] = low
        return totals + lax.dot_general(
            zs_ref[chunk], xy_ref[chunk], (((1,), (1,)), ((), ())), preferred_element_type=jnp.float32
        )

    totals = lax.fori_loop(0, chunk_count, factors, jnp.zeros((2 * rows, 128), jnp.float32), unroll=8)
    totals = totals[0:rows] + totals[rows : 2 * rows]
    totals = totals + pltpu.roll(totals, 64, 1)
    weight = weight_ref[...]
    ratio = jnp.concatenate([weight, weight], axis=1) / totals
    lanes = lax.broadcasted_iota(jnp.int32, (rows, 128), 1)
    step_x = (((lanes >> 3) & 7).astype(jnp.float32) - 3.5) / 8.0
    step_y = ((lanes & 7).astype(jnp.float32) - 3.5) / 8.0
    high, low = split(jnp.concatenate([ratio, ratio * step_x, ratio * step_y], axis=0))
    left = jnp.concatenate([high, low], axis=1)
    pixel_z = jnp.concatenate([step8 + (base_z + t) for t in range(tiles)], axis=0)

    def over_pixels(value):
        value = value.reshape(tiles, 8, 128)
        return jnp.sum(jnp.sum(value, axis=0), axis=0, keepdims=True)

    def moments(chunk, carry):
        right = xy_ref[chunk]
        pulled = jnp.dot(left, jnp.concatenate([right, right], axis=0), preferred_element_type=jnp.float32)
        for i in range(CHUNK):
            block = chunk * CHUNK + i
            cols = slice(i * 128, (i + 1) * 128)
            za = za_ref[block]
            share = za * pulled[0:rows, cols]
            mass = over_pixels(share)
            sum_z = over_pixels(share * pixel_z)
            sum_x = over_pixels(za * pulled[rows : 2 * rows, cols])
            sum_y = over_pixels(za * pulled[2 * rows : 3 * rows, cols])
            off_x, off_y = near(block)
            out_ref[block, 0:1, :] = mass
            out_ref[block, 1:2, :] = sum_x - off_x * mass
            out_ref[block, 2:3, :] = sum_y - off_y * mass
            out_ref[block, 3:4, :] = sum_z - seeds_ref[block, 2:3, :] * mass
        return carry

    lax.fori_loop(0, chunk_count, moments, 0, unroll=8)


def body(seed_data, block_slot, candidates, cand_count, pixel_mass):
    shard_index = lax.axis_index("seed")
    brick_size = lax.axis_size("brick")
    seed_size = lax.axis_size("seed")
    device_count = brick_size * seed_size
    lane_count = seed_data.shape[1] // 128
    home_blocks = lane_count * seed_size
    tile_count = candidates.shape[0]
    tiles = tile_count // seed_size
    assert tiles * seed_size == tile_count and TILES_Z % tiles == 0
    assert 128 % home_blocks == 0 and lane_count & (lane_count - 1) == 0
    assert device_count % CHUNK == 0
    sizes = (brick_size, seed_size, lane_count, home_blocks)
    vmem = pl.BlockSpec(memory_space=pltpu.VMEM)
    smem = pl.BlockSpec(memory_space=pltpu.SMEM)
    panel = pltpu.VMEM((device_count, 4, 128), jnp.float32)
    near = functools.partial(pltpu.with_memory_space_constraint, memory_space=pltpu.VMEM)
    params = pltpu.CompilerParams(vmem_limit_bytes=60 << 20)

    slots = block_slot.reshape(-1, 128)
    outgoing = pl.pallas_call(
        functools.partial(pack_kernel, sizes),
        out_shape=panel,
        in_specs=[vmem, vmem],
        out_specs=vmem,
        name="pack_seeds",
    )(slots, seed_data)
    incoming = lax.all_to_all(outgoing, ("brick", "seed"), split_axis=0, concat_axis=0, tiled=True)

    own = candidates.T
    panels = [own]
    for turn in range(1, seed_size):
        pairs = [(shard, (shard - turn) % seed_size) for shard in range(seed_size)]
        panels.append(lax.ppermute(own, "seed", pairs))
    slot_total = own.shape[0] * seed_size
    source, homes = pl.pallas_call(
        functools.partial(prepare_kernel, sizes, tiles),
        out_shape=(pltpu.VMEM((slot_total, tiles, 128), jnp.int32), pltpu.SMEM((lane_count,), jnp.int32)),
        in_specs=[vmem] * (2 + seed_size),
        out_specs=(vmem, smem),
        name="prepare",
    )(near(slots), near(cand_count.reshape(1, -1)), *[near(part) for part in panels])
    weight = lax.dynamic_slice_in_dim(pixel_mass, shard_index * tiles, tiles)
    weight = weight.reshape(tiles, 64, 8).transpose(0, 2, 1).reshape(tiles * 8, 64)

    partial = pl.pallas_call(
        functools.partial(main_kernel, tiles),
        out_shape=panel,
        in_specs=[vmem, vmem, vmem],
        out_specs=vmem,
        scratch_shapes=[
            pltpu.VMEM((device_count, tiles, 128), jnp.float32),
            pltpu.VMEM((device_count, tiles * 8, 128), jnp.float32),
            pltpu.VMEM((device_count // CHUNK, tiles * 16, CHUNK * 128), jnp.bfloat16),
            pltpu.VMEM((device_count // CHUNK, 128, CHUNK * 128), jnp.bfloat16),
        ],
        compiler_params=params,
        name="brick_moments",
    )(near(source), near(weight), near(incoming))
    returned = lax.all_to_all(partial, ("brick", "seed"), split_axis=0, concat_axis=0, tiled=True)
    return pl.pallas_call(
        functools.partial(place_kernel, seed_size),
        out_shape=jax.ShapeDtypeStruct(seed_data.shape, jnp.float32),
        in_specs=[smem, vmem],
        out_specs=vmem,
        name="place_stats",
    )(homes, near(returned))


def solution(mesh):
    placed = (P(None, ("brick", "seed")), P(), P("brick", "seed"), P("brick"), P("brick", None))
    return jax.shard_map(
        body, mesh=mesh, in_specs=placed, out_specs=P(None, ("brick", "seed")), check_vma=False
    )
```

```python
import functools

import jax
import jax.numpy as jnp
from jax import lax
from jax.experimental import pallas as pl
from jax.experimental.pallas import tpu as pltpu
from jax.sharding import PartitionSpec as P

TILES_Y = 2
TILES_Z = 8

LOG2E = 1.4426950408889634
LIFT = 40.0
DEAD = -1e30
CHUNK = 4


def stored_lane(slots, home, lane_count, home_blocks, device_index):
    per_row = 128 // home_blocks
    row = slots[home // per_row : home // per_row + 1, :]
    lanes = lax.broadcasted_iota(jnp.int32, (1, 128), 1)
    shift = lane_count.bit_length() - 1
    first = (home % per_row) * home_blocks
    found = (row >> shift == device_index) & (lanes >= first) & (lanes < first + home_blocks)
    return jnp.max(jnp.where(found, row & (lane_count - 1), -1))


def pack_kernel(sizes, slots_hbm, seeds_hbm, out_ref, slots_ref, seeds_ref, sems):
    brick_size, seed_size, lane_count, home_blocks = sizes
    device_index = lax.axis_index("brick") * seed_size + lax.axis_index("seed")
    fetch_slots = pltpu.make_async_copy(slots_hbm, slots_ref, sems.at[0])
    fetch_seeds = pltpu.make_async_copy(seeds_hbm, seeds_ref, sems.at[1])
    fetch_slots.start()
    fetch_seeds.start()
    fetch_slots.wait()
    slots = slots_ref[...]
    lanes = [stored_lane(slots, home, lane_count, home_blocks, device_index) for home in range(brick_size)]
    fetch_seeds.wait()
    for home in range(brick_size):
        first = pl.multiple_of(jnp.maximum(lanes[home], 0) * 128, 128)
        block = jnp.where(lanes[home] >= 0, seeds_ref[:, pl.ds(first, 128)], 0.0)
        for shard in range(seed_size):
            out_ref[home * seed_size + shard] = block


def prepare_kernel(sizes, tiles, slots_ref, counts_ref, *refs):
    brick_size, seed_size, lane_count, home_blocks = sizes
    panels, (source_ref, homes_ref) = refs[:seed_size], refs[seed_size:]
    brick_index = lax.axis_index("brick")
    shard_index = lax.axis_index("seed")
    shift = lane_count.bit_length() - 1
    slot_count, tile_count = panels[0].shape

    row = brick_index // (128 // home_blocks)
    lanes = lax.broadcasted_iota(jnp.int32, (1, 128), 1)
    ident = jnp.broadcast_to(row * 128 + lanes, (tiles, 128))
    holder = jnp.broadcast_to(slots_ref[pl.ds(row, 1), :] >> shift, (tiles, 128))
    mine = shard_index * tiles + lax.broadcasted_iota(jnp.int32, (tiles, tile_count), 0)
    mine = mine == lax.broadcasted_iota(jnp.int32, (tiles, tile_count), 1)
    counts = counts_ref[...]
    for turn in range(seed_size):
        shard = lax.rem(shard_index + turn, seed_size)
        for k in range(slot_count):
            chosen = jnp.where(shard * slot_count + k < counts, panels[turn][k : k + 1, :], -1)
            chosen = jnp.where(mine, jnp.broadcast_to(chosen, (tiles, tile_count)), -1)
            chosen = jnp.max(chosen, axis=1, keepdims=True)
            source = jnp.max(jnp.where(ident == chosen, holder, -1), axis=1, keepdims=True)
            source_ref[turn * slot_count + k] = jnp.broadcast_to(source, (tiles, 128))

    slots = slots_ref[...]
    rows = lax.broadcasted_iota(jnp.int32, slots.shape, 0)
    lanes = lax.broadcasted_iota(jnp.int32, slots.shape, 1)
    home = (rows * 128 + lanes) >> (home_blocks.bit_length() - 1)
    first = (brick_index * seed_size + shard_index) * lane_count
    for lane in range(lane_count):
        homes_ref[lane] = jnp.max(jnp.where(slots == first + lane, home, 0))


def place_kernel(seed_size, homes_ref, partial_ref, out_ref):
    for lane in range(out_ref.shape[1] // 128):
        first = homes_ref[lane] * seed_size
        block = partial_ref[first]
        for shard in range(1, seed_size):
            block = block + partial_ref[first + shard]
        out_ref[:, lane * 128 : (lane + 1) * 128] = block


def split(value):
    high = value.astype(jnp.bfloat16)
    low = (value - high.astype(jnp.float32)).astype(jnp.bfloat16)
    return high, low


def main_kernel(tiles, source_ref, weight_ref, seeds_ref, out_ref, score_ref, za_ref, zs_ref, xy_ref, lift_ref):
    source_count = seeds_ref.shape[0]
    slot_count = source_ref.shape[0]
    chunk_count = source_count // CHUNK
    rows = tiles * 8
    first_tile = lax.axis_index("seed") * tiles
    tile_x = first_tile // (TILES_Y * TILES_Z)
    tile_y = lax.axis_index("brick") * TILES_Y + first_tile // TILES_Z % TILES_Y
    tile_z = first_tile % TILES_Z
    centre_x = tile_x.astype(jnp.float32) + 0.5
    centre_y = tile_y.astype(jnp.float32) + 0.5
    base_z = tile_z.astype(jnp.float32) + 0.5
    centre_z = base_z + lax.broadcasted_iota(jnp.int32, (tiles, 128), 0).astype(jnp.float32)
    step8 = (lax.broadcasted_iota(jnp.int32, (8, 128), 0).astype(jnp.float32) - 3.5) / 8.0

    shift_z = [jnp.exp2(step8 * (-4.0 * LOG2E * t)) for t in range(tiles)]

    slot_source = [source_ref[k] for k in range(slot_count)]

    def near(block):
        off_x = jnp.clip(seeds_ref[block, 0:1, :] - centre_x, -8.0, 8.0)
        off_y = jnp.clip(seeds_ref[block, 1:2, :] - centre_y, -8.0, 8.0)
        return off_x, off_y

    def centre_scores(block, peak):
        off_x, off_y = near(block)
        off_z = seeds_ref[block, 2:3, :] - centre_z
        score = (seeds_ref[block, 3:4, :] - (off_x * off_x + off_y * off_y)) - off_z * off_z
        live = slot_source[0] == block
        for k in range(1, slot_count):
            live = live | (slot_source[k] == block)
        score = jnp.where(live, score, DEAD)
        score_ref[block] = score
        return jnp.maximum(peak, score)

    peak = lax.fori_loop(
        0, source_count, centre_scores, jnp.full((tiles, 128), DEAD, jnp.float32), unroll=8
    )
    peak = jnp.max(peak, axis=1, keepdims=True)

    def factors(chunk, totals):
        for i in range(CHUNK):
            block = chunk * CHUNK + i
            cols = slice(i * 128, (i + 1) * 128)
            off_x, off_y = near(block)
            lift = jnp.exp2((score_ref[block] - peak) * (2.0 * LOG2E) + LIFT * LOG2E)
            pull_z = jnp.exp2(step8 * ((seeds_ref[block, 2:3, :] - base_z) * (4.0 * LOG2E)))
            za = jnp.concatenate(
                [(pull_z * shift_z[t]) * lift[t : t + 1] for t in range(tiles)], axis=0
            )
            za_ref[block] = za
            high, low = split(za)
            zs_ref[chunk, 0:rows, cols] = high
            zs_ref[chunk, rows : 2 * rows, cols] = low
            slope_x = off_x * (0.5 * LOG2E)
            part_y = step8 * (off_y * (4.0 * LOG2E))
            grow = jnp.broadcast_to(jnp.exp2(slope_x), (8, 128))
            plane = [jnp.exp2(part_y - 3.5 * slope_x)]
            for ix in range(1, 8):
                plane.append(plane[-1] * grow)
            xy = jnp.concatenate(plane, axis=0)
            high, low = split(xy)
            xy_ref[chunk, 0:64, cols] = high
            xy_ref[chunk, 64:128, cols] = low
        return totals + lax.dot_general(
            zs_ref[chunk], xy_ref[chunk], (((1,), (1,)), ((), ())), preferred_element_type=jnp.float32
        )

    totals = lax.fori_loop(0, chunk_count, factors, jnp.zeros((2 * rows, 128), jnp.float32), unroll=8)
    totals = totals[0:rows] + totals[rows : 2 * rows]
    totals = totals + pltpu.roll(totals, 64, 1)
    weight = weight_ref[...]
    ratio = jnp.concatenate([weight, weight], axis=1) / totals
    lanes = lax.broadcasted_iota(jnp.int32, (rows, 128), 1)
    step_x = (((lanes >> 3) & 7).astype(jnp.float32) - 3.5) / 8.0
    step_y = ((lanes & 7).astype(jnp.float32) - 3.5) / 8.0
    high, low = split(jnp.concatenate([ratio, ratio * step_x, ratio * step_y], axis=0))
    left = jnp.concatenate([high, low], axis=1)
    pixel_z = jnp.concatenate([step8 + (base_z + t) for t in range(tiles)], axis=0)

    def over_pixels(value):
        value = value.reshape(tiles, 8, 128)
        return jnp.sum(jnp.sum(value, axis=0), axis=0, keepdims=True)

    def moments(chunk, carry):
        right = xy_ref[chunk]
        pulled = jnp.dot(left, jnp.concatenate([right, right], axis=0), preferred_element_type=jnp.float32)
        for i in range(CHUNK):
            block = chunk * CHUNK + i
            cols = slice(i * 128, (i + 1) * 128)
            za = za_ref[block]
            share = za * pulled[0:rows, cols]
            mass = over_pixels(share)
            sum_z = over_pixels(share * pixel_z)
            sum_x = over_pixels(za * pulled[rows : 2 * rows, cols])
            sum_y = over_pixels(za * pulled[2 * rows : 3 * rows, cols])
            off_x, off_y = near(block)
            out_ref[block, 0:1, :] = mass
            out_ref[block, 1:2, :] = sum_x - off_x * mass
            out_ref[block, 2:3, :] = sum_y - off_y * mass
            out_ref[block, 3:4, :] = sum_z - seeds_ref[block, 2:3, :] * mass
        return carry

    lax.fori_loop(0, chunk_count, moments, 0, unroll=8)


def body(seed_data, block_slot, candidates, cand_count, pixel_mass):
    shard_index = lax.axis_index("seed")
    brick_size = lax.axis_size("brick")
    seed_size = lax.axis_size("seed")
    device_count = brick_size * seed_size
    lane_count = seed_data.shape[1] // 128
    home_blocks = lane_count * seed_size
    tile_count = candidates.shape[0]
    tiles = tile_count // seed_size
    assert tiles * seed_size == tile_count and TILES_Z % tiles == 0
    assert 128 % home_blocks == 0 and lane_count & (lane_count - 1) == 0
    assert device_count % CHUNK == 0
    sizes = (brick_size, seed_size, lane_count, home_blocks)
    vmem = pl.BlockSpec(memory_space=pltpu.VMEM)
    smem = pl.BlockSpec(memory_space=pltpu.SMEM)
    hbm = pl.BlockSpec(memory_space=pltpu.HBM)
    panel = pltpu.VMEM((device_count, 4, 128), jnp.float32)
    near = functools.partial(pltpu.with_memory_space_constraint, memory_space=pltpu.VMEM)
    params = pltpu.CompilerParams(vmem_limit_bytes=60 << 20)

    slots = block_slot.reshape(-1, 128)
    outgoing = pl.pallas_call(
        functools.partial(pack_kernel, sizes),
        out_shape=panel,
        in_specs=[hbm, hbm],
        out_specs=vmem,
        scratch_shapes=[
            pltpu.VMEM(slots.shape, slots.dtype),
            pltpu.VMEM(seed_data.shape, seed_data.dtype),
            pltpu.SemaphoreType.DMA((2,)),
        ],
        name="pack_seeds",
    )(slots, seed_data)
    incoming = lax.all_to_all(outgoing, ("brick", "seed"), split_axis=0, concat_axis=0, tiled=True)

    own = candidates.T
    panels = [own]
    for turn in range(1, seed_size):
        pairs = [(shard, (shard - turn) % seed_size) for shard in range(seed_size)]
        panels.append(lax.ppermute(own, "seed", pairs))
    slot_total = own.shape[0] * seed_size
    source, homes = pl.pallas_call(
        functools.partial(prepare_kernel, sizes, tiles),
        out_shape=(pltpu.VMEM((slot_total, tiles, 128), jnp.int32), pltpu.SMEM((lane_count,), jnp.int32)),
        in_specs=[vmem] * (2 + seed_size),
        out_specs=(vmem, smem),
        name="prepare",
    )(near(slots), near(cand_count.reshape(1, -1)), *[near(part) for part in panels])
    weight = lax.dynamic_slice_in_dim(pixel_mass, shard_index * tiles, tiles)
    weight = weight.reshape(tiles, 64, 8).transpose(0, 2, 1).reshape(tiles * 8, 64)

    partial = pl.pallas_call(
        functools.partial(main_kernel, tiles),
        out_shape=panel,
        in_specs=[vmem, vmem, vmem],
        out_specs=vmem,
        scratch_shapes=[
            pltpu.VMEM((device_count, tiles, 128), jnp.float32),
            pltpu.VMEM((device_count, tiles * 8, 128), jnp.float32),
            pltpu.VMEM((device_count // CHUNK, tiles * 16, CHUNK * 128), jnp.bfloat16),
            pltpu.VMEM((device_count // CHUNK, 128, CHUNK * 128), jnp.bfloat16),
            pltpu.VMEM((CHUNK, tiles, 128), jnp.float32),
        ],
        compiler_params=params,
        name="brick_moments",
    )(near(source), near(weight), near(incoming))
    returned = lax.all_to_all(partial, ("brick", "seed"), split_axis=0, concat_axis=0, tiled=True)
    return pl.pallas_call(
        functools.partial(place_kernel, seed_size),
        out_shape=jax.ShapeDtypeStruct(seed_data.shape, jnp.float32),
        in_specs=[smem, vmem],
        out_specs=vmem,
        name="place_stats",
    )(homes, near(returned))


def solution(mesh):
    placed = (P(None, ("brick", "seed")), P(), P("brick", "seed"), P("brick"), P("brick", None))
    return jax.shard_map(
        body, mesh=mesh, in_specs=placed, out_specs=P(None, ("brick", "seed")), check_vma=False
    )
```

```python
import functools

import jax
import jax.numpy as jnp
from jax import lax
from jax.experimental import pallas as pl
from jax.experimental.pallas import tpu as pltpu
from jax.sharding import PartitionSpec as P

TILES_Y = 2
TILES_Z = 8

LOG2E = 1.4426950408889634
LIFT = 40.0
DEAD = -1e30
CHUNK = 4


def stored_lane(slots, home, lane_count, home_blocks, device_index):
    per_row = 128 // home_blocks
    row = slots[home // per_row : home // per_row + 1, :]
    lanes = lax.broadcasted_iota(jnp.int32, (1, 128), 1)
    shift = lane_count.bit_length() - 1
    first = (home % per_row) * home_blocks
    found = (row >> shift == device_index) & (lanes >= first) & (lanes < first + home_blocks)
    return jnp.max(jnp.where(found, row & (lane_count - 1), -1))


def pack_kernel(sizes, slots_hbm, seeds_hbm, out_ref, slots_ref, seeds_ref, sems):
    brick_size, seed_size, lane_count, home_blocks = sizes
    device_index = lax.axis_index("brick") * seed_size + lax.axis_index("seed")
    fetch_slots = pltpu.make_async_copy(slots_hbm, slots_ref, sems.at[0])
    fetch_seeds = pltpu.make_async_copy(seeds_hbm, seeds_ref, sems.at[1])
    fetch_slots.start()
    fetch_seeds.start()
    fetch_slots.wait()
    slots = slots_ref[...]
    lanes = [stored_lane(slots, home, lane_count, home_blocks, device_index) for home in range(brick_size)]
    fetch_seeds.wait()
    for home in range(brick_size):
        first = pl.multiple_of(jnp.maximum(lanes[home], 0) * 128, 128)
        block = jnp.where(lanes[home] >= 0, seeds_ref[:, pl.ds(first, 128)], 0.0)
        for shard in range(seed_size):
            out_ref[home * seed_size + shard] = block


def prepare_kernel(sizes, tiles, slots_ref, counts_ref, *refs):
    brick_size, seed_size, lane_count, home_blocks = sizes
    panels, (source_ref, homes_ref) = refs[:seed_size], refs[seed_size:]
    brick_index = lax.axis_index("brick")
    shard_index = lax.axis_index("seed")
    shift = lane_count.bit_length() - 1
    slot_count, tile_count = panels[0].shape

    row = brick_index // (128 // home_blocks)
    lanes = lax.broadcasted_iota(jnp.int32, (1, 128), 1)
    ident = jnp.broadcast_to(row * 128 + lanes, (tiles, 128))
    holder = jnp.broadcast_to(slots_ref[pl.ds(row, 1), :] >> shift, (tiles, 128))
    mine = shard_index * tiles + lax.broadcasted_iota(jnp.int32, (tiles, tile_count), 0)
    mine = mine == lax.broadcasted_iota(jnp.int32, (tiles, tile_count), 1)
    counts = counts_ref[...]
    words = [jnp.zeros((tiles, 128), jnp.int32)] * source_ref.shape[0]
    for turn in range(seed_size):
        shard = lax.rem(shard_index + turn, seed_size)
        for k in range(slot_count):
            chosen = jnp.where(shard * slot_count + k < counts, panels[turn][k : k + 1, :], -1)
            chosen = jnp.where(mine, jnp.broadcast_to(chosen, (tiles, tile_count)), -1)
            chosen = jnp.max(chosen, axis=1, keepdims=True)
            source = jnp.max(jnp.where(ident == chosen, holder, -1), axis=1, keepdims=True)
            source = jnp.broadcast_to(source, (tiles, 128))
            bit = jnp.where(source >= 0, jnp.left_shift(1, source & 31), 0)
            for word in range(len(words)):
                words[word] = words[word] | jnp.where(source >> 5 == word, bit, 0)
    for word in range(len(words)):
        source_ref[word] = words[word]

    slots = slots_ref[...]
    rows = lax.broadcasted_iota(jnp.int32, slots.shape, 0)
    lanes = lax.broadcasted_iota(jnp.int32, slots.shape, 1)
    home = (rows * 128 + lanes) >> (home_blocks.bit_length() - 1)
    first = (brick_index * seed_size + shard_index) * lane_count
    for lane in range(lane_count):
        homes_ref[lane] = jnp.max(jnp.where(slots == first + lane, home, 0))


def place_kernel(seed_size, homes_ref, partial_ref, out_ref):
    for lane in range(out_ref.shape[1] // 128):
        first = homes_ref[lane] * seed_size
        block = partial_ref[first]
        for shard in range(1, seed_size):
            block = block + partial_ref[first + shard]
        out_ref[:, lane * 128 : (lane + 1) * 128] = block


def split(value):
    high = value.astype(jnp.bfloat16)
    low = (value - high.astype(jnp.float32)).astype(jnp.bfloat16)
    return high, low


def main_kernel(tiles, source_ref, weight_ref, seeds_ref, out_ref, score_ref, zs_ref, xy_ref):
    source_count = seeds_ref.shape[0]
    chunk_count = source_count // CHUNK
    rows = tiles * 8
    first_tile = lax.axis_index("seed") * tiles
    tile_x = first_tile // (TILES_Y * TILES_Z)
    tile_y = lax.axis_index("brick") * TILES_Y + first_tile // TILES_Z % TILES_Y
    tile_z = first_tile % TILES_Z
    centre_x = tile_x.astype(jnp.float32) + 0.5
    centre_y = tile_y.astype(jnp.float32) + 0.5
    base_z = tile_z.astype(jnp.float32) + 0.5
    centre_z = base_z + lax.broadcasted_iota(jnp.int32, (tiles, 128), 0).astype(jnp.float32)
    step8 = (lax.broadcasted_iota(jnp.int32, (8, 128), 0).astype(jnp.float32) - 3.5) / 8.0

    shift_z = [jnp.exp2(step8 * (-4.0 * LOG2E * t)) for t in range(tiles)]


    def near(block):
        off_x = jnp.clip(seeds_ref[block, 0:1, :] - centre_x, -8.0, 8.0)
        off_y = jnp.clip(seeds_ref[block, 1:2, :] - centre_y, -8.0, 8.0)
        return off_x, off_y

    def centre_scores(word, peak):
        bits = source_ref[word]
        for i in range(32):
            block = word * 32 + i
            off_x, off_y = near(block)
            off_z = seeds_ref[block, 2:3, :] - centre_z
            score = (seeds_ref[block, 3:4, :] - (off_x * off_x + off_y * off_y)) - off_z * off_z
            score = jnp.where((bits >> i) & 1 == 1, score, DEAD)
            score_ref[block] = score
            peak = jnp.maximum(peak, score)
        return peak

    peak = lax.fori_loop(0, source_count // 32, centre_scores, jnp.full((tiles, 128), DEAD, jnp.float32))
    peak = jnp.max(peak, axis=1, keepdims=True)

    def factors(chunk, totals):
        planes, columns = [], []
        for i in range(CHUNK):
            block = chunk * CHUNK + i
            off_x, off_y = near(block)
            lift = jnp.exp2((score_ref[block] - peak) * (2.0 * LOG2E) + LIFT * LOG2E)
            pull_z = jnp.exp2(step8 * ((seeds_ref[block, 2:3, :] - base_z) * (4.0 * LOG2E)))
            za = jnp.concatenate([(pull_z * shift_z[t]) * lift[t : t + 1] for t in range(tiles)], axis=0)
            both = jnp.concatenate(split(za), axis=0)
            zs_ref[chunk, :, i * 128 : (i + 1) * 128] = both
            columns.append(both)
            slope_x = off_x * (0.5 * LOG2E)
            part_y = step8 * (off_y * (4.0 * LOG2E))
            grow = jnp.broadcast_to(jnp.exp2(slope_x), (8, 128))
            plane = [jnp.exp2(part_y - 3.5 * slope_x)]
            for ix in range(1, 8):
                plane.append(plane[-1] * grow)
            xy = jnp.concatenate(plane, axis=0)
            xy_ref[block] = xy
            planes.append(jnp.concatenate(split(xy), axis=0))
        dot = functools.partial(
            lax.dot_general, dimension_numbers=(((1,), (1,)), ((), ())), preferred_element_type=jnp.float32
        )
        half = CHUNK // 2
        first = dot(jnp.concatenate(planes[:half], axis=1), jnp.concatenate(columns[:half], axis=1))
        second = dot(jnp.concatenate(planes[half:], axis=1), jnp.concatenate(columns[half:], axis=1))
        return totals[0] + first, totals[1] + second

    totals = lax.fori_loop(0, chunk_count, factors, (jnp.zeros((128, 2 * rows), jnp.float32),) * 2, unroll=8)
    totals = totals[0] + totals[1]
    totals = totals[0:64] + totals[64:128]
    totals = totals[:, 0:rows] + totals[:, rows : 2 * rows]
    ratio = weight_ref[...] / totals
    ratio = jnp.concatenate([ratio, ratio], axis=1)
    lanes = lax.broadcasted_iota(jnp.int32, (64, 2 * rows), 1) & (rows - 1)
    pixel_z = base_z + (lanes >> 3).astype(jnp.float32) + ((lanes & 7).astype(jnp.float32) - 3.5) / 8.0
    left = jnp.concatenate(split(jnp.concatenate([ratio, ratio * pixel_z], axis=0)), axis=1)

    def over_rows(value):
        return jnp.sum(value, axis=0, keepdims=True)

    def moments(chunk, carry):
        right = zs_ref[chunk]
        pulled = jnp.dot(left, jnp.concatenate([right, right], axis=0), preferred_element_type=jnp.float32)
        for i in range(CHUNK):
            block = chunk * CHUNK + i
            cols = slice(i * 128, (i + 1) * 128)
            xy = xy_ref[block]
            share = [xy[ix * 8 : ix * 8 + 8] * pulled[ix * 8 : ix * 8 + 8, cols] for ix in range(8)]
            total = share[7]
            ramp = share[7]
            for ix in range(6, 0, -1):
                total = total + share[ix]
                ramp = ramp + total
            total = total + share[0]
            mass = over_rows(total)
            sum_x = over_rows(ramp) * 0.125 - mass * (3.5 / 8.0)
            sum_y = over_rows(total * step8)
            sum_z = over_rows(jnp.sum((xy * pulled[64:128, cols]).reshape(8, 8, 128), axis=0))
            off_x, off_y = near(block)
            out_ref[block, 0:1, :] = mass
            out_ref[block, 1:2, :] = sum_x - off_x * mass
            out_ref[block, 2:3, :] = sum_y - off_y * mass
            out_ref[block, 3:4, :] = sum_z - seeds_ref[block, 2:3, :] * mass
        return carry

    lax.fori_loop(0, chunk_count, moments, 0, unroll=8)


def body(seed_data, block_slot, candidates, cand_count, pixel_mass):
    shard_index = lax.axis_index("seed")
    brick_size = lax.axis_size("brick")
    seed_size = lax.axis_size("seed")
    device_count = brick_size * seed_size
    lane_count = seed_data.shape[1] // 128
    home_blocks = lane_count * seed_size
    tile_count = candidates.shape[0]
    tiles = tile_count // seed_size
    assert tiles * seed_size == tile_count and TILES_Z % tiles == 0
    assert 128 % home_blocks == 0 and lane_count & (lane_count - 1) == 0
    assert device_count % 32 == 0 and 32 % CHUNK == 0
    sizes = (brick_size, seed_size, lane_count, home_blocks)
    vmem = pl.BlockSpec(memory_space=pltpu.VMEM)
    smem = pl.BlockSpec(memory_space=pltpu.SMEM)
    hbm = pl.BlockSpec(memory_space=pltpu.HBM)
    panel = pltpu.VMEM((device_count, 4, 128), jnp.float32)
    near = functools.partial(pltpu.with_memory_space_constraint, memory_space=pltpu.VMEM)
    params = pltpu.CompilerParams(vmem_limit_bytes=60 << 20)

    slots = block_slot.reshape(-1, 128)
    outgoing = pl.pallas_call(
        functools.partial(pack_kernel, sizes),
        out_shape=panel,
        in_specs=[hbm, hbm],
        out_specs=vmem,
        scratch_shapes=[
            pltpu.VMEM(slots.shape, slots.dtype),
            pltpu.VMEM(seed_data.shape, seed_data.dtype),
            pltpu.SemaphoreType.DMA((2,)),
        ],
        name="pack_seeds",
    )(slots, seed_data)
    incoming = lax.all_to_all(outgoing, ("brick", "seed"), split_axis=0, concat_axis=0, tiled=True)

    own = candidates.T
    panels = [own]
    for turn in range(1, seed_size):
        pairs = [(shard, (shard - turn) % seed_size) for shard in range(seed_size)]
        panels.append(lax.ppermute(own, "seed", pairs))
    source, homes = pl.pallas_call(
        functools.partial(prepare_kernel, sizes, tiles),
        out_shape=(pltpu.VMEM((device_count // 32, tiles, 128), jnp.int32), pltpu.SMEM((lane_count,), jnp.int32)),
        in_specs=[vmem] * (2 + seed_size),
        out_specs=(vmem, smem),
        name="prepare",
    )(near(slots), near(cand_count.reshape(1, -1)), *[near(part) for part in panels])
    weight = lax.dynamic_slice_in_dim(pixel_mass, shard_index * tiles, tiles)
    weight = weight.reshape(tiles, 64, 8).transpose(1, 0, 2).reshape(64, tiles * 8)

    partial = pl.pallas_call(
        functools.partial(main_kernel, tiles),
        out_shape=panel,
        in_specs=[vmem, vmem, vmem],
        out_specs=vmem,
        scratch_shapes=[
            pltpu.VMEM((device_count, tiles, 128), jnp.float32),
            pltpu.VMEM((device_count // CHUNK, tiles * 16, CHUNK * 128), jnp.bfloat16),
            pltpu.VMEM((device_count, 64, 128), jnp.float32),
        ],
        compiler_params=params,
        name="brick_moments",
    )(near(source), near(weight), near(incoming))
    returned = lax.all_to_all(partial, ("brick", "seed"), split_axis=0, concat_axis=0, tiled=True)
    return pl.pallas_call(
        functools.partial(place_kernel, seed_size),
        out_shape=jax.ShapeDtypeStruct(seed_data.shape, jnp.float32),
        in_specs=[smem, vmem],
        out_specs=vmem,
        name="place_stats",
    )(homes, near(returned))


def solution(mesh):
    placed = (P(None, ("brick", "seed")), P(), P("brick", "seed"), P("brick"), P("brick", None))
    return jax.shard_map(
        body, mesh=mesh, in_specs=placed, out_specs=P(None, ("brick", "seed")), check_vma=False
    )
```

```python
import functools

import jax
import jax.numpy as jnp
from jax import lax
from jax.experimental import pallas as pl
from jax.experimental.pallas import tpu as pltpu
from jax.sharding import PartitionSpec as P

TILES_Y = 2
TILES_Z = 8

LOG2E = 1.4426950408889634
LIFT = 40.0
DEAD = -1e30
CHUNK = 4


def stored_lane(slots, home, lane_count, home_blocks, device_index):
    per_row = 128 // home_blocks
    row = slots[home // per_row : home // per_row + 1, :]
    lanes = lax.broadcasted_iota(jnp.int32, (1, 128), 1)
    shift = lane_count.bit_length() - 1
    first = (home % per_row) * home_blocks
    found = (row >> shift == device_index) & (lanes >= first) & (lanes < first + home_blocks)
    return jnp.max(jnp.where(found, row & (lane_count - 1), -1))


def pack_kernel(sizes, slots_hbm, seeds_hbm, out_ref, slots_ref, seeds_ref, sems):
    brick_size, seed_size, lane_count, home_blocks = sizes
    device_index = lax.axis_index("brick") * seed_size + lax.axis_index("seed")
    fetch_slots = pltpu.make_async_copy(slots_hbm, slots_ref, sems.at[0])
    fetch_seeds = pltpu.make_async_copy(seeds_hbm, seeds_ref, sems.at[1])
    fetch_slots.start()
    fetch_seeds.start()
    fetch_slots.wait()
    slots = slots_ref[...]
    lanes = [stored_lane(slots, home, lane_count, home_blocks, device_index) for home in range(brick_size)]
    fetch_seeds.wait()
    for home in range(brick_size):
        first = pl.multiple_of(jnp.maximum(lanes[home], 0) * 128, 128)
        block = jnp.where(lanes[home] >= 0, seeds_ref[:, pl.ds(first, 128)], 0.0)
        for shard in range(seed_size):
            out_ref[shard * brick_size + home] = block


def prepare_kernel(sizes, tiles, slots_ref, counts_ref, *refs):
    brick_size, seed_size, lane_count, home_blocks = sizes
    panels, (source_ref, homes_ref) = refs[:seed_size], refs[seed_size:]
    brick_index = lax.axis_index("brick")
    shard_index = lax.axis_index("seed")
    shift = lane_count.bit_length() - 1
    slot_count, tile_count = panels[0].shape

    row = brick_index // (128 // home_blocks)
    lanes = lax.broadcasted_iota(jnp.int32, (1, 128), 1)
    ident = jnp.broadcast_to(row * 128 + lanes, (tiles, 128))
    holder = slots_ref[pl.ds(row, 1), :] >> shift
    holder = (holder & (seed_size - 1)) * brick_size + (holder >> (seed_size.bit_length() - 1))
    holder = jnp.broadcast_to(holder, (tiles, 128))
    mine = shard_index * tiles + lax.broadcasted_iota(jnp.int32, (tiles, tile_count), 0)
    mine = mine == lax.broadcasted_iota(jnp.int32, (tiles, tile_count), 1)
    counts = counts_ref[...]
    words = [jnp.zeros((tiles, 128), jnp.int32)] * source_ref.shape[0]
    for turn in range(seed_size):
        shard = lax.rem(shard_index + turn, seed_size)
        for k in range(slot_count):
            chosen = jnp.where(shard * slot_count + k < counts, panels[turn][k : k + 1, :], -1)
            chosen = jnp.where(mine, jnp.broadcast_to(chosen, (tiles, tile_count)), -1)
            chosen = jnp.max(chosen, axis=1, keepdims=True)
            source = jnp.max(jnp.where(ident == chosen, holder, -1), axis=1, keepdims=True)
            source = jnp.broadcast_to(source, (tiles, 128))
            bit = jnp.where(source >= 0, jnp.left_shift(1, source & 31), 0)
            for word in range(len(words)):
                words[word] = words[word] | jnp.where(source >> 5 == word, bit, 0)
    for word in range(len(words)):
        source_ref[word] = words[word]

    slots = slots_ref[...]
    rows = lax.broadcasted_iota(jnp.int32, slots.shape, 0)
    lanes = lax.broadcasted_iota(jnp.int32, slots.shape, 1)
    home = (rows * 128 + lanes) >> (home_blocks.bit_length() - 1)
    first = (brick_index * seed_size + shard_index) * lane_count
    for lane in range(lane_count):
        homes_ref[lane] = jnp.max(jnp.where(slots == first + lane, home, 0))


def place_kernel(brick_size, seed_size, homes_ref, partial_ref, out_ref):
    for lane in range(out_ref.shape[1] // 128):
        home = homes_ref[lane]
        block = partial_ref[home]
        for shard in range(1, seed_size):
            block = block + partial_ref[shard * brick_size + home]
        out_ref[:, lane * 128 : (lane + 1) * 128] = block


def split(value):
    high = value.astype(jnp.bfloat16)
    low = (value - high.astype(jnp.float32)).astype(jnp.bfloat16)
    return high, low


def main_kernel(tiles, source_ref, weight_ref, seeds_ref, out_ref, score_ref, zs_ref, xy_ref):
    source_count = seeds_ref.shape[0]
    chunk_count = source_count // CHUNK
    rows = tiles * 8
    first_tile = lax.axis_index("seed") * tiles
    tile_x = first_tile // (TILES_Y * TILES_Z)
    tile_y = lax.axis_index("brick") * TILES_Y + first_tile // TILES_Z % TILES_Y
    tile_z = first_tile % TILES_Z
    centre_x = tile_x.astype(jnp.float32) + 0.5
    centre_y = tile_y.astype(jnp.float32) + 0.5
    base_z = tile_z.astype(jnp.float32) + 0.5
    centre_z = base_z + lax.broadcasted_iota(jnp.int32, (tiles, 128), 0).astype(jnp.float32)
    step8 = (lax.broadcasted_iota(jnp.int32, (8, 128), 0).astype(jnp.float32) - 3.5) / 8.0

    shift_z = [jnp.exp2(step8 * (-4.0 * LOG2E * t)) for t in range(tiles)]


    def near(block):
        off_x = jnp.clip(seeds_ref[block, 0:1, :] - centre_x, -8.0, 8.0)
        off_y = jnp.clip(seeds_ref[block, 1:2, :] - centre_y, -8.0, 8.0)
        return off_x, off_y

    def centre_scores(word, peak):
        bits = source_ref[word]
        for i in range(32):
            block = word * 32 + i
            off_x, off_y = near(block)
            off_z = seeds_ref[block, 2:3, :] - centre_z
            score = (seeds_ref[block, 3:4, :] - (off_x * off_x + off_y * off_y)) - off_z * off_z
            score = jnp.where((bits >> i) & 1 == 1, score, DEAD)
            score_ref[block] = score
            peak = jnp.maximum(peak, score)
        return peak

    peak = lax.fori_loop(0, source_count // 32, centre_scores, jnp.full((tiles, 128), DEAD, jnp.float32))
    peak = jnp.max(peak, axis=1, keepdims=True)

    def factors(chunk, totals):
        planes, columns = [], []
        for i in range(CHUNK):
            block = chunk * CHUNK + i
            off_x, off_y = near(block)
            lift = jnp.exp2((score_ref[block] - peak) * (2.0 * LOG2E) + LIFT * LOG2E)
            pull_z = jnp.exp2(step8 * ((seeds_ref[block, 2:3, :] - base_z) * (4.0 * LOG2E)))
            za = jnp.concatenate([(pull_z * shift_z[t]) * lift[t : t + 1] for t in range(tiles)], axis=0)
            both = jnp.concatenate(split(za), axis=0)
            zs_ref[chunk, :, i * 128 : (i + 1) * 128] = both
            columns.append(both)
            slope_x = off_x * (0.5 * LOG2E)
            part_y = step8 * (off_y * (4.0 * LOG2E))
            grow = jnp.broadcast_to(jnp.exp2(slope_x), (8, 128))
            plane = [jnp.exp2(part_y - 3.5 * slope_x)]
            for ix in range(1, 8):
                plane.append(plane[-1] * grow)
            xy = jnp.concatenate(plane, axis=0)
            xy_ref[block] = xy
            planes.append(jnp.concatenate(split(xy), axis=0))
        dot = functools.partial(
            lax.dot_general, dimension_numbers=(((1,), (1,)), ((), ())), preferred_element_type=jnp.float32
        )
        half = CHUNK // 2
        first = dot(jnp.concatenate(planes[:half], axis=1), jnp.concatenate(columns[:half], axis=1))
        second = dot(jnp.concatenate(planes[half:], axis=1), jnp.concatenate(columns[half:], axis=1))
        return totals[0] + first, totals[1] + second

    totals = lax.fori_loop(0, chunk_count, factors, (jnp.zeros((128, 2 * rows), jnp.float32),) * 2, unroll=8)
    totals = totals[0] + totals[1]
    totals = totals[0:64] + totals[64:128]
    totals = totals[:, 0:rows] + totals[:, rows : 2 * rows]
    ratio = weight_ref[...] / totals
    ratio = jnp.concatenate([ratio, ratio], axis=1)
    lanes = lax.broadcasted_iota(jnp.int32, (64, 2 * rows), 1) & (rows - 1)
    pixel_z = base_z + (lanes >> 3).astype(jnp.float32) + ((lanes & 7).astype(jnp.float32) - 3.5) / 8.0
    left = jnp.concatenate(split(jnp.concatenate([ratio, ratio * pixel_z], axis=0)), axis=1)

    def over_rows(value):
        return jnp.sum(value, axis=0, keepdims=True)

    def moments(chunk, carry):
        right = zs_ref[chunk]
        pulled = jnp.dot(left, jnp.concatenate([right, right], axis=0), preferred_element_type=jnp.float32)
        for i in range(CHUNK):
            block = chunk * CHUNK + i
            cols = slice(i * 128, (i + 1) * 128)
            xy = xy_ref[block]
            share = [xy[ix * 8 : ix * 8 + 8] * pulled[ix * 8 : ix * 8 + 8, cols] for ix in range(8)]
            total = share[7]
            ramp = share[7]
            for ix in range(6, 0, -1):
                total = total + share[ix]
                ramp = ramp + total
            total = total + share[0]
            mass = over_rows(total)
            sum_x = over_rows(ramp) * 0.125 - mass * (3.5 / 8.0)
            sum_y = over_rows(total * step8)
            sum_z = over_rows(jnp.sum((xy * pulled[64:128, cols]).reshape(8, 8, 128), axis=0))
            off_x, off_y = near(block)
            out_ref[block, 0:1, :] = mass
            out_ref[block, 1:2, :] = sum_x - off_x * mass
            out_ref[block, 2:3, :] = sum_y - off_y * mass
            out_ref[block, 3:4, :] = sum_z - seeds_ref[block, 2:3, :] * mass
        return carry

    lax.fori_loop(0, chunk_count, moments, 0, unroll=8)


def body(seed_data, block_slot, candidates, cand_count, pixel_mass):
    shard_index = lax.axis_index("seed")
    brick_size = lax.axis_size("brick")
    seed_size = lax.axis_size("seed")
    device_count = brick_size * seed_size
    lane_count = seed_data.shape[1] // 128
    home_blocks = lane_count * seed_size
    tile_count = candidates.shape[0]
    tiles = tile_count // seed_size
    assert tiles * seed_size == tile_count and TILES_Z % tiles == 0
    assert seed_size & (seed_size - 1) == 0
    assert 128 % home_blocks == 0 and lane_count & (lane_count - 1) == 0
    assert device_count % 32 == 0 and 32 % CHUNK == 0
    sizes = (brick_size, seed_size, lane_count, home_blocks)
    vmem = pl.BlockSpec(memory_space=pltpu.VMEM)
    smem = pl.BlockSpec(memory_space=pltpu.SMEM)
    hbm = pl.BlockSpec(memory_space=pltpu.HBM)
    panel = pltpu.VMEM((device_count, 4, 128), jnp.float32)
    near = functools.partial(pltpu.with_memory_space_constraint, memory_space=pltpu.VMEM)
    params = pltpu.CompilerParams(vmem_limit_bytes=60 << 20)

    slots = block_slot.reshape(-1, 128)
    outgoing = pl.pallas_call(
        functools.partial(pack_kernel, sizes),
        out_shape=panel,
        in_specs=[hbm, hbm],
        out_specs=vmem,
        scratch_shapes=[
            pltpu.VMEM(slots.shape, slots.dtype),
            pltpu.VMEM(seed_data.shape, seed_data.dtype),
            pltpu.SemaphoreType.DMA((2,)),
        ],
        name="pack_seeds",
    )(slots, seed_data)
    incoming = lax.all_to_all(outgoing, ("seed", "brick"), split_axis=0, concat_axis=0, tiled=True)

    own = candidates.T
    panels = [own]
    for turn in range(1, seed_size):
        pairs = [(shard, (shard - turn) % seed_size) for shard in range(seed_size)]
        panels.append(lax.ppermute(own, "seed", pairs))
    source, homes = pl.pallas_call(
        functools.partial(prepare_kernel, sizes, tiles),
        out_shape=(pltpu.VMEM((device_count // 32, tiles, 128), jnp.int32), pltpu.SMEM((lane_count,), jnp.int32)),
        in_specs=[vmem] * (2 + seed_size),
        out_specs=(vmem, smem),
        name="prepare",
    )(near(slots), near(cand_count.reshape(1, -1)), *[near(part) for part in panels])
    weight = lax.dynamic_slice_in_dim(pixel_mass, shard_index * tiles, tiles)
    weight = weight.reshape(tiles, 64, 8).transpose(1, 0, 2).reshape(64, tiles * 8)

    partial = pl.pallas_call(
        functools.partial(main_kernel, tiles),
        out_shape=panel,
        in_specs=[vmem, vmem, vmem],
        out_specs=vmem,
        scratch_shapes=[
            pltpu.VMEM((device_count, tiles, 128), jnp.float32),
            pltpu.VMEM((device_count // CHUNK, tiles * 16, CHUNK * 128), jnp.bfloat16),
            pltpu.VMEM((device_count, 64, 128), jnp.float32),
        ],
        compiler_params=params,
        name="brick_moments",
    )(near(source), near(weight), near(incoming))
    returned = lax.all_to_all(partial, ("seed", "brick"), split_axis=0, concat_axis=0, tiled=True)
    return pl.pallas_call(
        functools.partial(place_kernel, brick_size, seed_size),
        out_shape=jax.ShapeDtypeStruct(seed_data.shape, jnp.float32),
        in_specs=[smem, vmem],
        out_specs=vmem,
        name="place_stats",
    )(homes, near(returned))


def solution(mesh):
    placed = (P(None, ("brick", "seed")), P(), P("brick", "seed"), P("brick"), P("brick", None))
    return jax.shard_map(
        body, mesh=mesh, in_specs=placed, out_specs=P(None, ("brick", "seed")), check_vma=False
    )
```

```python
import functools

import jax
import jax.numpy as jnp
from jax import lax
from jax.experimental import pallas as pl
from jax.experimental.pallas import tpu as pltpu
from jax.sharding import PartitionSpec as P

TILES_Y = 2
TILES_Z = 8

LOG2E = 1.4426950408889634
LIFT = 40.0
DEAD = -1e30
CHUNK = 8


def stored_lane(slots, home, lane_count, home_blocks, device_index):
    per_row = 128 // home_blocks
    row = slots[home // per_row : home // per_row + 1, :]
    lanes = lax.broadcasted_iota(jnp.int32, (1, 128), 1)
    shift = lane_count.bit_length() - 1
    first = (home % per_row) * home_blocks
    found = (row >> shift == device_index) & (lanes >= first) & (lanes < first + home_blocks)
    return jnp.max(jnp.where(found, row & (lane_count - 1), -1))


def pack_kernel(sizes, slots_hbm, seeds_hbm, out_ref, slots_ref, seeds_ref, sems):
    brick_size, seed_size, lane_count, home_blocks = sizes
    device_index = lax.axis_index("brick") * seed_size + lax.axis_index("seed")
    fetch_slots = pltpu.make_async_copy(slots_hbm, slots_ref, sems.at[0])
    fetch_seeds = pltpu.make_async_copy(seeds_hbm, seeds_ref, sems.at[1])
    fetch_slots.start()
    fetch_seeds.start()
    fetch_slots.wait()
    slots = slots_ref[...]
    lanes = [stored_lane(slots, home, lane_count, home_blocks, device_index) for home in range(brick_size)]
    fetch_seeds.wait()
    for home in range(brick_size):
        first = pl.multiple_of(jnp.maximum(lanes[home], 0) * 128, 128)
        block = jnp.where(lanes[home] >= 0, seeds_ref[:, pl.ds(first, 128)], 0.0)
        for shard in range(seed_size):
            out_ref[shard * brick_size + home] = block


def prepare_kernel(sizes, tiles, slots_ref, counts_ref, *refs):
    brick_size, seed_size, lane_count, home_blocks = sizes
    panels, (source_ref, homes_ref) = refs[:seed_size], refs[seed_size:]
    brick_index = lax.axis_index("brick")
    shard_index = lax.axis_index("seed")
    shift = lane_count.bit_length() - 1
    slot_count, tile_count = panels[0].shape

    row = brick_index // (128 // home_blocks)
    lanes = lax.broadcasted_iota(jnp.int32, (1, 128), 1)
    ident = jnp.broadcast_to(row * 128 + lanes, (tiles, 128))
    holder = slots_ref[pl.ds(row, 1), :] >> shift
    holder = (holder & (seed_size - 1)) * brick_size + (holder >> (seed_size.bit_length() - 1))
    holder = jnp.broadcast_to(holder, (tiles, 128))
    mine = shard_index * tiles + lax.broadcasted_iota(jnp.int32, (tiles, tile_count), 0)
    mine = mine == lax.broadcasted_iota(jnp.int32, (tiles, tile_count), 1)
    counts = counts_ref[...]
    words = [jnp.zeros((tiles, 128), jnp.int32)] * source_ref.shape[0]
    for turn in range(seed_size):
        shard = lax.rem(shard_index + turn, seed_size)
        for k in range(slot_count):
            chosen = jnp.where(shard * slot_count + k < counts, panels[turn][k : k + 1, :], -1)
            chosen = jnp.where(mine, jnp.broadcast_to(chosen, (tiles, tile_count)), -1)
            chosen = jnp.max(chosen, axis=1, keepdims=True)
            source = jnp.max(jnp.where(ident == chosen, holder, -1), axis=1, keepdims=True)
            source = jnp.broadcast_to(source, (tiles, 128))
            bit = jnp.where(source >= 0, jnp.left_shift(1, source & 31), 0)
            for word in range(len(words)):
                words[word] = words[word] | jnp.where(source >> 5 == word, bit, 0)
    for word in range(len(words)):
        source_ref[word] = words[word]

    slots = slots_ref[...]
    rows = lax.broadcasted_iota(jnp.int32, slots.shape, 0)
    lanes = lax.broadcasted_iota(jnp.int32, slots.shape, 1)
    home = (rows * 128 + lanes) >> (home_blocks.bit_length() - 1)
    first = (brick_index * seed_size + shard_index) * lane_count
    for lane in range(lane_count):
        homes_ref[lane] = jnp.max(jnp.where(slots == first + lane, home, 0))


def place_kernel(brick_size, seed_size, homes_ref, partial_ref, out_ref):
    for lane in range(out_ref.shape[1] // 128):
        home = homes_ref[lane]
        block = partial_ref[home]
        for shard in range(1, seed_size):
            block = block + partial_ref[shard * brick_size + home]
        out_ref[:, lane * 128 : (lane + 1) * 128] = block


def split(value):
    high = value.astype(jnp.bfloat16)
    low = (value - high.astype(jnp.float32)).astype(jnp.bfloat16)
    return high, low


def main_kernel(tiles, source_ref, weight_ref, seeds_ref, out_ref, score_ref, zs_ref, xy_ref):
    source_count = seeds_ref.shape[0]
    chunk_count = source_count // CHUNK
    rows = tiles * 8
    first_tile = lax.axis_index("seed") * tiles
    tile_x = first_tile // (TILES_Y * TILES_Z)
    tile_y = lax.axis_index("brick") * TILES_Y + first_tile // TILES_Z % TILES_Y
    tile_z = first_tile % TILES_Z
    centre_x = tile_x.astype(jnp.float32) + 0.5
    centre_y = tile_y.astype(jnp.float32) + 0.5
    base_z = tile_z.astype(jnp.float32) + 0.5
    centre_z = base_z + lax.broadcasted_iota(jnp.int32, (tiles, 128), 0).astype(jnp.float32)
    step8 = (lax.broadcasted_iota(jnp.int32, (8, 128), 0).astype(jnp.float32) - 3.5) / 8.0

    shift_z = [jnp.exp2(step8 * (-4.0 * LOG2E * t)) for t in range(tiles)]


    def near(block):
        off_x = jnp.clip(seeds_ref[block, 0:1, :] - centre_x, -8.0, 8.0)
        off_y = jnp.clip(seeds_ref[block, 1:2, :] - centre_y, -8.0, 8.0)
        return off_x, off_y

    def centre_scores(word, peak):
        bits = source_ref[word]
        for i in range(32):
            block = word * 32 + i
            off_x, off_y = near(block)
            off_z = seeds_ref[block, 2:3, :] - centre_z
            score = (seeds_ref[block, 3:4, :] - (off_x * off_x + off_y * off_y)) - off_z * off_z
            score = jnp.where((bits >> i) & 1 == 1, score, DEAD)
            score_ref[block] = score
            peak = jnp.maximum(peak, score)
        return peak

    peak = lax.fori_loop(0, source_count // 32, centre_scores, jnp.full((tiles, 128), DEAD, jnp.float32))
    peak = jnp.max(peak, axis=1, keepdims=True)

    def factors(chunk, totals):
        planes, columns = [], []
        for i in range(CHUNK):
            block = chunk * CHUNK + i
            off_x, off_y = near(block)
            lift = jnp.exp2((score_ref[block] - peak) * (2.0 * LOG2E) + LIFT * LOG2E)
            pull_z = jnp.exp2(step8 * ((seeds_ref[block, 2:3, :] - base_z) * (4.0 * LOG2E)))
            za = jnp.concatenate([(pull_z * shift_z[t]) * lift[t : t + 1] for t in range(tiles)], axis=0)
            both = jnp.concatenate(split(za), axis=0)
            zs_ref[chunk, :, i * 128 : (i + 1) * 128] = both
            columns.append(both)
            slope_x = off_x * (0.5 * LOG2E)
            part_y = step8 * (off_y * (4.0 * LOG2E))
            grow = jnp.broadcast_to(jnp.exp2(slope_x), (8, 128))
            plane = [jnp.exp2(part_y - 3.5 * slope_x)]
            for ix in range(1, 8):
                plane.append(plane[-1] * grow)
            xy = jnp.concatenate(plane, axis=0)
            xy_ref[block] = xy
            planes.append(jnp.concatenate(split(xy), axis=0))
        dot = functools.partial(
            lax.dot_general, dimension_numbers=(((1,), (1,)), ((), ())), preferred_element_type=jnp.float32
        )
        half = CHUNK // 2
        first = dot(jnp.concatenate(planes[:half], axis=1), jnp.concatenate(columns[:half], axis=1))
        second = dot(jnp.concatenate(planes[half:], axis=1), jnp.concatenate(columns[half:], axis=1))
        return totals[0] + first, totals[1] + second

    totals = lax.fori_loop(0, chunk_count, factors, (jnp.zeros((128, 2 * rows), jnp.float32),) * 2, unroll=4)
    totals = totals[0] + totals[1]
    totals = totals[0:64] + totals[64:128]
    totals = totals[:, 0:rows] + totals[:, rows : 2 * rows]
    ratio = weight_ref[...] / totals
    ratio = jnp.concatenate([ratio, ratio], axis=1)
    lanes = lax.broadcasted_iota(jnp.int32, (64, 2 * rows), 1) & (rows - 1)
    pixel_z = base_z + (lanes >> 3).astype(jnp.float32) + ((lanes & 7).astype(jnp.float32) - 3.5) / 8.0
    left = jnp.concatenate(split(jnp.concatenate([ratio, ratio * pixel_z], axis=0)), axis=1)

    def over_rows(value):
        return jnp.sum(value, axis=0, keepdims=True)

    def moments(chunk, carry):
        right = zs_ref[chunk]
        pulled = jnp.dot(left, jnp.concatenate([right, right], axis=0), preferred_element_type=jnp.float32)
        for i in range(CHUNK):
            block = chunk * CHUNK + i
            cols = slice(i * 128, (i + 1) * 128)
            xy = xy_ref[block]
            share = [xy[ix * 8 : ix * 8 + 8] * pulled[ix * 8 : ix * 8 + 8, cols] for ix in range(8)]
            total = share[7]
            ramp = share[7]
            for ix in range(6, 0, -1):
                total = total + share[ix]
                ramp = ramp + total
            total = total + share[0]
            mass = over_rows(total)
            sum_x = over_rows(ramp) * 0.125 - mass * (3.5 / 8.0)
            sum_y = over_rows(total * step8)
            sum_z = over_rows(jnp.sum((xy * pulled[64:128, cols]).reshape(8, 8, 128), axis=0))
            off_x, off_y = near(block)
            out_ref[block, 0:1, :] = mass
            out_ref[block, 1:2, :] = sum_x - off_x * mass
            out_ref[block, 2:3, :] = sum_y - off_y * mass
            out_ref[block, 3:4, :] = sum_z - seeds_ref[block, 2:3, :] * mass
        return carry

    lax.fori_loop(0, chunk_count, moments, 0, unroll=4)


def body(seed_data, block_slot, candidates, cand_count, pixel_mass):
    shard_index = lax.axis_index("seed")
    brick_size = lax.axis_size("brick")
    seed_size = lax.axis_size("seed")
    device_count = brick_size * seed_size
    lane_count = seed_data.shape[1] // 128
    home_blocks = lane_count * seed_size
    tile_count = candidates.shape[0]
    tiles = tile_count // seed_size
    assert tiles * seed_size == tile_count and TILES_Z % tiles == 0
    assert seed_size & (seed_size - 1) == 0
    assert 128 % home_blocks == 0 and lane_count & (lane_count - 1) == 0
    assert device_count % 32 == 0 and 32 % CHUNK == 0
    sizes = (brick_size, seed_size, lane_count, home_blocks)
    vmem = pl.BlockSpec(memory_space=pltpu.VMEM)
    smem = pl.BlockSpec(memory_space=pltpu.SMEM)
    hbm = pl.BlockSpec(memory_space=pltpu.HBM)
    panel = pltpu.VMEM((device_count, 4, 128), jnp.float32)
    near = functools.partial(pltpu.with_memory_space_constraint, memory_space=pltpu.VMEM)
    params = pltpu.CompilerParams(vmem_limit_bytes=60 << 20)

    slots = block_slot.reshape(-1, 128)
    outgoing = pl.pallas_call(
        functools.partial(pack_kernel, sizes),
        out_shape=panel,
        in_specs=[hbm, hbm],
        out_specs=vmem,
        scratch_shapes=[
            pltpu.VMEM(slots.shape, slots.dtype),
            pltpu.VMEM(seed_data.shape, seed_data.dtype),
            pltpu.SemaphoreType.DMA((2,)),
        ],
        name="pack_seeds",
    )(slots, seed_data)
    incoming = lax.all_to_all(outgoing, ("seed", "brick"), split_axis=0, concat_axis=0, tiled=True)

    own = candidates.T
    panels = [own]
    for turn in range(1, seed_size):
        pairs = [(shard, (shard - turn) % seed_size) for shard in range(seed_size)]
        panels.append(lax.ppermute(own, "seed", pairs))
    source, homes = pl.pallas_call(
        functools.partial(prepare_kernel, sizes, tiles),
        out_shape=(pltpu.VMEM((device_count // 32, tiles, 128), jnp.int32), pltpu.SMEM((lane_count,), jnp.int32)),
        in_specs=[vmem] * (2 + seed_size),
        out_specs=(vmem, smem),
        name="prepare",
    )(near(slots), near(cand_count.reshape(1, -1)), *[near(part) for part in panels])
    weight = lax.dynamic_slice_in_dim(pixel_mass, shard_index * tiles, tiles)
    weight = weight.reshape(tiles, 64, 8).transpose(1, 0, 2).reshape(64, tiles * 8)

    partial = pl.pallas_call(
        functools.partial(main_kernel, tiles),
        out_shape=panel,
        in_specs=[vmem, vmem, vmem],
        out_specs=vmem,
        scratch_shapes=[
            pltpu.VMEM((device_count, tiles, 128), jnp.float32),
            pltpu.VMEM((device_count // CHUNK, tiles * 16, CHUNK * 128), jnp.bfloat16),
            pltpu.VMEM((device_count, 64, 128), jnp.float32),
        ],
        compiler_params=params,
        name="brick_moments",
    )(near(source), near(weight), near(incoming))
    returned = lax.all_to_all(partial, ("seed", "brick"), split_axis=0, concat_axis=0, tiled=True)
    return pl.pallas_call(
        functools.partial(place_kernel, brick_size, seed_size),
        out_shape=jax.ShapeDtypeStruct(seed_data.shape, jnp.float32),
        in_specs=[smem, vmem],
        out_specs=vmem,
        name="place_stats",
    )(homes, near(returned))


def solution(mesh):
    placed = (P(None, ("brick", "seed")), P(), P("brick", "seed"), P("brick"), P("brick", None))
    return jax.shard_map(
        body, mesh=mesh, in_specs=placed, out_specs=P(None, ("brick", "seed")), check_vma=False
    )
```
